512 devices in a mesh: cam: 32 (over z, x_lo), row: 16 (over y, x_hi, core).
Axes of the slice: x: 4 (x_hi: 2, x_lo: 2; x = x_hi * 2 + x_lo), y: 4, z: 16, core: 2. Of those that a mesh axis runs over, the one named last changes fastest.
Arguments:
- features_in: bfloat16 [32, 64, 128, 128], P('cam', 'row'), may hold values from -6 to 6
- conv_weight: bfloat16 [3, 3, 128, 128], replicated, may hold values from -0.1875 to 0.1875
- q_weight: bfloat16 [128, 128], replicated, may hold values from -0.5 to 0.5
- k_weight: bfloat16 [128, 128], replicated, may hold values from -0.5 to 0.5
- v_weight: bfloat16 [128, 128], replicated, may hold values from -0.5 to 0.5
- partners: int32 [32, 2], replicated, may hold values from 0 to 31, as said below
- band_widths: int32 [32, 2], replicated, may hold values from 1 to 3, as said below
- bands: int32 [32, 64, 2, 3], P('cam', 'row'), may hold values from 0 to 63, as said below
- grad_attended: bfloat16 [32, 64, 128, 128], P('cam', 'row'), may hold values from -6 to 6
Outputs:
- attended: bfloat16 [32, 64, 128, 128], P('cam', 'row')
- grad_features: bfloat16 [32, 64, 128, 128], P('cam', 'row')
The draws below stay inside these ranges and needn't reach their ends.
Inputs may be any that keep to these rules, and one draw needn't show every extreme that they name: `partners`: view c is camera c // 2 of sample c % 2; partner 0 of view c is view c - 2 or c - 4 and partner 1 is view c + 2 or c + 4, modulo 32, so both are cameras of the same sample next or next but one in the cyclic order of its 16 cameras. `band_widths`: some view and partner have 3 live slots and some have 1. `bands`: entries are block numbers of the partner view; a block is one image row, so the block number is the image row; the 3 entries of a list are distinct and lie in image rows 4 * s - 2 to 4 * (s + 1) + 1, where s is the query block's image row // 4.
All inputs are finite; a program needn't handle non-finite values.
Results may differ from the reference program's by a relative error of at most 0.011.
Values may be sent and summed in bfloat16 or wider, within the bound.
A program may use at most 64 MiB of HBM per device.

```python
import jax
import jax.numpy as jnp
from jax import lax

CHANNELS = 128
WIDTH = 128
BLOCK = 128
ROWS_DEV = 4
MARGIN = 2
BAND = 3
SAMPLES = 2
VIEWS = 32
HEIGHT = 64
QBLOCKS = 64


def draw_features_in(key, part):
    noise_key = jax.random.fold_in(key, 41)
    shape = (VIEWS, HEIGHT, WIDTH, CHANNELS)
    return jax.random.truncated_normal(noise_key, -6.0, 6.0, shape, jnp.float32).astype(jnp.bfloat16)


def draw_partners(key, part):
    gap_key = jax.random.fold_in(key, 11)
    gaps = jax.random.randint(gap_key, (VIEWS, 2), 1, 3)
    cameras = jnp.arange(VIEWS, dtype=jnp.int32)
    before_cam = jnp.mod(cameras - gaps[:, 0] * SAMPLES, VIEWS)
    after_cam = jnp.mod(cameras + gaps[:, 1] * SAMPLES, VIEWS)
    return jnp.stack([before_cam, after_cam], axis=1).astype(jnp.int32)


def draw_band_widths(key, part):
    width_key = jax.random.fold_in(key, 21)
    pick_key = jax.random.fold_in(key, 22)
    flat = jax.random.randint(width_key, (2 * VIEWS,), 1, BAND + 1)
    chosen = jax.random.randint(pick_key, (), 0, 2 * VIEWS)
    places = jnp.arange(2 * VIEWS, dtype=jnp.int32)
    flat = jnp.where(places == chosen, BAND, flat)
    flat = jnp.where(places == jnp.mod(chosen + 1, 2 * VIEWS), 1, flat)
    return flat.reshape(VIEWS, 2).astype(jnp.int32)


def draw_bands(key, part):
    step_key = jax.random.fold_in(key, 31)
    start_key = jax.random.fold_in(key, 32)
    per_row = WIDTH // BLOCK
    block_ids = jnp.arange(QBLOCKS, dtype=jnp.int32)
    slab = block_ids // per_row // ROWS_DEV
    low = jnp.maximum(slab * ROWS_DEV - MARGIN, 0) * per_row
    high = jnp.minimum((slab + 1) * ROWS_DEV + MARGIN, HEIGHT) * per_row
    stride = jnp.where(jax.random.randint(step_key, (VIEWS, QBLOCKS, 2), 0, 2) == 1, per_row, 1)
    room = high[None, :, None] - low[None, :, None] - (BAND - 1) * stride
    start = low[None, :, None] + jnp.mod(jax.random.randint(start_key, (VIEWS, QBLOCKS, 2), 0, 1048576), room)
    offsets = jnp.arange(BAND, dtype=jnp.int32)
    return (start[..., None] + stride[..., None] * offsets).astype(jnp.int32)


def block_scale(key, extent, cuts, low, top_value):
    level, own = 1.0, jax.random.fold_in(key, 6)
    for dim, blocks in cuts:
        heights = jnp.exp(jax.random.uniform(jax.random.fold_in(own, dim), (blocks,), jnp.float32, low / len(cuts), top_value / len(cuts)))
        level = level * jnp.repeat(heights, extent[dim] // blocks).reshape([-1 if axis == dim else 1 for axis in range(len(extent))])
    return level


def normal_values(rng, dims, spread, bound, cuts=(), kind=jnp.bfloat16):
    drawn = jax.random.normal(rng, dims, jnp.float32) * spread
    if len(cuts) > 0:
        drawn = block_scale(rng, dims, cuts, -0.22, 0.18) * drawn
    return jnp.clip(drawn, min=-bound, max=bound).astype(kind)


def setup_inputs(seed: int = 0) -> dict:
    arg_keys = jax.random.split(jax.random.key(seed), 10)
    features_in = draw_features_in(jax.random.fold_in(arg_keys[9], 71), 0)
    conv_weight = normal_values(arg_keys[1], (3, 3, CHANNELS, CHANNELS), (9 * CHANNELS) ** -0.5, 0.1875)
    q_weight = normal_values(arg_keys[2], (CHANNELS, CHANNELS), CHANNELS ** -0.5, 0.5)
    k_weight = normal_values(arg_keys[3], (CHANNELS, CHANNELS), CHANNELS ** -0.5, 0.5)
    v_weight = normal_values(arg_keys[4], (CHANNELS, CHANNELS), CHANNELS ** -0.5, 0.5)
    partners = draw_partners(jax.random.fold_in(arg_keys[9], 71), 0)
    band_widths = draw_band_widths(jax.random.fold_in(arg_keys[9], 71), 0)
    bands = draw_bands(jax.random.fold_in(arg_keys[9], 71), 0)
    grad_attended = normal_values(arg_keys[8], (VIEWS, HEIGHT, WIDTH, CHANNELS), 1.0, 6.0, ((0, 32), (1, 16)))
    return {"features_in": features_in, "conv_weight": conv_weight, "q_weight": q_weight, "k_weight": k_weight, "v_weight": v_weight, "partners": partners, "band_widths": band_widths, "bands": bands, "grad_attended": grad_attended}


def reference(features_in, conv_weight, q_weight, k_weight, v_weight, partners, band_widths, bands, grad_attended):
    channels = CHANNELS
    inverse_square_root = channels ** -0.5
    high = lax.Precision.HIGHEST

    def project(image):
        hidden = lax.conv_general_dilated(image[None].astype(jnp.float32), conv_weight.astype(jnp.float32), (1, 1), ((1, 1), (1, 1)), dimension_numbers=("NHWC", "HWIO", "NHWC"), precision=high)[0]
        hidden = hidden.astype(jnp.bfloat16).reshape(HEIGHT * WIDTH, channels)
        queries = jnp.dot(hidden, q_weight, preferred_element_type=jnp.float32).astype(jnp.bfloat16)
        key_rows = jnp.dot(hidden, k_weight, preferred_element_type=jnp.float32).astype(jnp.bfloat16)
        value_rows = jnp.dot(hidden, v_weight, preferred_element_type=jnp.float32).astype(jnp.bfloat16)
        return queries, key_rows, value_rows

    all_q, all_k, all_v = lax.map(project, features_in)
    key_blocks = all_k.reshape(VIEWS, QBLOCKS, BLOCK, channels)
    value_blocks = all_v.reshape(VIEWS, QBLOCKS, BLOCK, channels)
    slots = jnp.arange(BAND, dtype=jnp.int32)
    back_weight = jnp.concatenate([k_weight, v_weight], axis=1).astype(jnp.float32).T
    query_back = q_weight.astype(jnp.float32).T
    key_count = 2 * BAND * BLOCK

    def one_view(camera, carry):
        attended, grad_acc = carry
        pair_row = partners[camera]
        widths_here = band_widths[camera]
        lists = bands[camera]
        key_rows = jnp.concatenate([key_blocks[pair_row[0]][lists[:, 0]], key_blocks[pair_row[1]][lists[:, 1]]], axis=1)
        key_rows = key_rows.reshape(QBLOCKS, key_count, channels).astype(jnp.float32)
        value_rows = jnp.concatenate([value_blocks[pair_row[0]][lists[:, 0]], value_blocks[pair_row[1]][lists[:, 1]]], axis=1)
        value_rows = value_rows.reshape(QBLOCKS, key_count, channels).astype(jnp.float32)
        live = jnp.repeat(jnp.concatenate([slots < widths_here[0], slots < widths_here[1]]), BLOCK)
        query_block = all_q[camera].reshape(QBLOCKS, BLOCK, channels).astype(jnp.float32)
        score_matrix = jnp.einsum("apx,anx->apn", query_block, key_rows) * inverse_square_root
        expo = jnp.where(live, jnp.exp(score_matrix), 0.0)
        probs = expo / jnp.sum(expo, axis=2, keepdims=True)
        probabilities_halfwidth = lax.optimization_barrier(probs.astype(jnp.bfloat16)).astype(jnp.float32)
        output_rows = jnp.einsum("zld,zdi->zli", probabilities_halfwidth, value_rows)
        attended = attended.at[camera].set(output_rows.astype(jnp.bfloat16))
        incoming_gradient = grad_attended[camera].reshape(QBLOCKS, BLOCK, channels).astype(jnp.float32)
        probability_gradient = jnp.einsum("apx,anx->apn", incoming_gradient, value_rows)
        delta = jnp.sum(probs * probability_gradient, axis=2, keepdims=True)
        score_gradient = lax.optimization_barrier((probs * (probability_gradient - delta)).astype(jnp.bfloat16)).astype(jnp.float32)
        query_gradient = jnp.einsum("zld,zdi->zli", score_gradient, key_rows) * inverse_square_root
        key_gradient = jnp.einsum("wds,wdm->wsm", score_gradient, query_block) * inverse_square_root
        value_gradient = jnp.einsum("wds,wdm->wsm", probabilities_halfwidth, incoming_gradient)
        grad_own = jnp.dot(query_gradient.reshape(-1, channels), query_back, precision=high)
        grad_acc = grad_acc.at[camera].add(grad_own.reshape(QBLOCKS, BLOCK, channels))
        pieces = jnp.dot(jnp.concatenate([key_gradient, value_gradient], axis=2).reshape(-1, 2 * channels), back_weight, precision=high)
        pieces = pieces.reshape(QBLOCKS, 2, BAND, BLOCK, channels)
        grad_acc = grad_acc.at[pair_row[0], lists[:, 0]].add(pieces[:, 0])
        grad_acc = grad_acc.at[pair_row[1], lists[:, 1]].add(pieces[:, 1])
        return attended, grad_acc

    start_att = jnp.zeros((VIEWS, QBLOCKS, BLOCK, channels), jnp.bfloat16)
    start_grad = jnp.zeros((VIEWS, QBLOCKS, BLOCK, channels), jnp.float32)
    attended, grad_acc = lax.fori_loop(0, VIEWS, one_view, (start_att, start_grad))
    attended = attended.reshape(VIEWS, HEIGHT, WIDTH, channels)
    grad_features = grad_acc.astype(jnp.bfloat16).reshape(VIEWS, HEIGHT, WIDTH, channels)
    return attended, grad_features
```

```python
import functools

import jax
import jax.numpy as jnp
from jax import lax
from jax.experimental import pallas as pl
from jax.experimental.pallas import tpu as pltpu
from jax.sharding import PartitionSpec as P

MESH = pl.DeviceIdType.MESH
BLOCK = 128
MARGIN = 2
BAND = 3
F32 = jnp.float32
BF16 = jnp.bfloat16

NN = (((1,), (0,)), ((), ()))
NT = (((1,), (1,)), ((), ()))
TN = (((0,), (0,)), ((), ()))


def dot(a, b, dims=NN):
    return lax.dot_general(a, b, dims, preferred_element_type=F32)


def kernel(
    views,
    slabs,
    feat,
    conv_w,
    q_w,
    k_w,
    v_w,
    partners,
    widths,
    bands,
    grad_att,
    att_out,
    grad_out,
    fbuf,
    wconv,
    wq,
    wk,
    wv,
    dabuf,
    hown,
    cand,
    wsel,
    qa,
    pd,
    att,
    own,
    acc,
    gmar,
    rmar,
    ztot,
    zin,
    gout,
    load_sem,
    halo_send,
    halo_recv,
    z_send,
    z_recv,
    m_send,
    m_recv,
    b_send,
    b_recv,
    y_send,
    y_recv,
    out_sem,
):
    step = views // min(16, views)
    rows = hown.shape[0]
    width, channels = hown.shape[1], hown.shape[2]
    cam = lax.axis_index("cam")
    slab = lax.axis_index("row")
    cam_r, cam_l = lax.rem(cam + step, views), lax.rem(cam + views - step, views)
    slab_n, slab_p = lax.rem(slab + 1, slabs), lax.rem(slab + slabs - 1, slabs)
    right, left = (cam_r, slab), (cam_l, slab)
    above, below = (cam, slab_p), (cam, slab_n)

    barrier = pltpu.get_barrier_semaphore()
    for peer in (right, left, above, below):
        pl.semaphore_signal(barrier, inc=1, device_id=peer, device_id_type=MESH)

    loads = [
        pltpu.make_async_copy(feat.at[0], fbuf.at[pl.ds(1, rows)], load_sem.at[0]),
        pltpu.make_async_copy(conv_w, wconv, load_sem.at[1]),
        pltpu.make_async_copy(grad_att.at[0], dabuf, load_sem.at[2]),
        pltpu.make_async_copy(v_w, wv, load_sem.at[3]),
        pltpu.make_async_copy(q_w, wq, load_sem.at[4]),
        pltpu.make_async_copy(k_w, wk, load_sem.at[5]),
    ]
    for load in loads:
        load.start()

    def remote(src, dst, send, recv, peer):
        return pltpu.make_async_remote_copy(
            src_ref=src, dst_ref=dst, send_sem=send, recv_sem=recv, device_id=peer, device_id_type=MESH
        )

    halo_up = remote(feat.at[0, 0], fbuf.at[rows + 1], halo_send.at[0], halo_recv.at[0], above)
    halo_down = remote(feat.at[0, rows - 1], fbuf.at[0], halo_send.at[1], halo_recv.at[1], below)

    def near(r):
        return (
            remote(hown.at[r], cand.at[0, r], z_send.at[0, r], z_recv.at[0, r], right),
            remote(hown.at[r], cand.at[2, r], z_send.at[2, r], z_recv.at[2, r], left),
        )

    def far(r):
        return (
            remote(cand.at[0, r], cand.at[1, r], z_send.at[1, r], z_recv.at[1, r], right),
            remote(cand.at[2, r], cand.at[3, r], z_send.at[3, r], z_recv.at[3, r], left),
        )

    def conv(taps):
        total = None
        for dy in range(3):
            weight = jnp.concatenate([wconv[dy, 0], wconv[dy, 1], wconv[dy, 2]], axis=1)
            part = dot(taps[dy], weight)
            total = part if total is None else total + part
        size = total.shape[0]
        pixel = lax.rem(lax.broadcasted_iota(jnp.int32, (size, channels), 0), width)
        before = pltpu.roll(total[:, :channels], 1, 0)
        after = pltpu.roll(total[:, 2 * channels :], size - 1, 0)
        out = total[:, channels : 2 * channels]
        out = out + jnp.where(pixel == 0, 0.0, before) + jnp.where(pixel == width - 1, 0.0, after)
        return out.astype(BF16)

    loads[0].wait()
    loads[1].wait()
    inner = conv([fbuf[pl.ds(1 + dy, rows - 2)].reshape((rows - 2) * width, channels) for dy in range(3)])
    hown[pl.ds(1, rows - 2)] = inner.reshape(rows - 2, width, channels)

    pl.semaphore_wait(barrier, 4)
    halo_up.start()
    halo_down.start()
    for r in range(1, rows - 1):
        for copy in near(r):
            copy.start()

    loads[2].wait()
    loads[3].wait()
    loads[4].wait()
    loads[5].wait()
    grad_v = dot(dabuf[...].reshape(rows * width, channels), wv[...], NT).astype(BF16)
    qa[:, pl.ds(width, width), :] = grad_v.reshape(rows, width, channels)
    pd[:, 2 * BAND] = jnp.zeros((rows, BLOCK, 2 * width), BF16)

    halo_up.wait_recv()
    halo_down.wait_recv()
    top = jnp.where(slab == 0, jnp.zeros((width, channels), BF16), fbuf[0])
    bottom = jnp.where(slab == slabs - 1, jnp.zeros((width, channels), BF16), fbuf[rows + 1])
    hown[0] = conv([top, fbuf[1], fbuf[2]])
    hown[rows - 1] = conv([fbuf[rows - 1], fbuf[rows], bottom])
    for r in (0, rows - 1):
        for copy in near(r):
            copy.start()
    order = [*range(1, rows - 1), 0, rows - 1]
    for r in order:
        for near_copy, far_copy in zip(near(r), far(r)):
            near_copy.wait_recv()
            far_copy.start()

    scale = channels**-0.5
    queries = dot(hown[...].reshape(rows * width, channels), wq[...]).astype(BF16)
    queries = (dot(queries, wk[...], NT) * scale).astype(BF16)
    qa[:, pl.ds(0, width), :] = queries.reshape(rows, width, channels)

    gap0 = lax.rem(cam - partners[cam, 0] + views, views)
    gap1 = lax.rem(partners[cam, 1] - cam + views, views)

    for r in order:
        for copy in far(r):
            copy.wait_recv()
        wsel[0, MARGIN + r] = jnp.where(gap0 == step, cand[0, r], cand[1, r])
        wsel[1, MARGIN + r] = jnp.where(gap1 == step, cand[2, r], cand[3, r])

    def margin(side):
        return (
            remote(
                wsel.at[side, pl.ds(MARGIN, MARGIN)],
                wsel.at[side, pl.ds(MARGIN + rows, MARGIN)],
                m_send.at[side, 0],
                m_recv.at[side, 0],
                above,
            ),
            remote(
                wsel.at[side, pl.ds(rows, MARGIN)],
                wsel.at[side, pl.ds(0, MARGIN)],
                m_send.at[side, 1],
                m_recv.at[side, 1],
                below,
            ),
        )

    margins = [*margin(0), *margin(1)]
    for copy in margins:
        copy.start()
    for copy in margins:
        copy.wait_recv()

    base = slab * rows - MARGIN

    def attend(q, carry):
        qa_here = qa[q]
        keys, exps, grads = [], [], []
        total, weighted = None, None
        for side in range(2):
            for slot in range(BAND):
                place = jnp.clip(bands[0, q, side, slot] - base, 0, rows + 2 * MARGIN - 1)
                block = wsel[side, place]
                both = dot(block, qa_here, NT)
                live = jnp.where(slot < widths[cam, side], 1.0, 0.0).astype(F32)
                expo = jnp.where(live > 0.0, jnp.exp(both[:, :width]), 0.0)
                grad = both[:, width:]
                keys.append(block)
                exps.append(expo)
                grads.append(grad)
                here = jnp.sum(expo, axis=0, keepdims=True)
                here_w = jnp.sum(expo * grad, axis=0, keepdims=True)
                total = here if total is None else total + here
                weighted = here_w if weighted is None else weighted + here_w
        inverse = 1.0 / total
        delta = weighted * inverse
        pairs = []
        for place in range(2 * BAND):
            prob = exps[place] * inverse
            score = prob * (grads[place] - delta)
            pair = jnp.concatenate([score.astype(BF16), prob.astype(BF16)], axis=1)
            pd[q, place] = pair
            pairs.append(pair)
        mixed = dot(jnp.concatenate(keys, axis=0), jnp.concatenate(pairs, axis=0), TN).astype(BF16)
        att[q] = dot(mixed[:, width:], wv[...], TN).astype(BF16)
        grad_q = (dot(mixed[:, :width], wk[...], TN) * scale).astype(BF16)
        own[q] = dot(grad_q, wq[...], NT)
        return carry

    lax.fori_loop(0, rows, attend, 0)

    att_copy = pltpu.make_async_copy(att, att_out.at[0], out_sem.at[0])
    att_copy.start()

    def place_of(q, side, row):
        place = jnp.int32(2 * BAND)
        for slot in range(BAND):
            place = jnp.where(bands[0, q, side, slot] - base == row, side * BAND + slot, place)
        return place

    def key_grads(which):
        summed = None
        for q in range(rows):
            lhs = jnp.concatenate([pd[q, place_of(q, side, row)] for side, row in which], axis=0)
            part = dot(lhs, qa[q])
            summed = part if summed is None else summed + part
        return summed.reshape(len(which), BLOCK, channels)

    upper = [(side, row) for side in range(2) for row in range(MARGIN)]
    lower = [(side, row) for side in range(2) for row in range(MARGIN + rows, 2 * MARGIN + rows)]
    gmar[...] = key_grads(upper + lower).astype(BF16).reshape(gmar.shape)
    back_up = remote(gmar.at[0], rmar.at[0], b_send.at[0], b_recv.at[0], above)
    back_down = remote(gmar.at[1], rmar.at[1], b_send.at[1], b_recv.at[1], below)
    back_up.start()
    back_down.start()
    middle = [(side, row) for side in range(2) for row in range(MARGIN, MARGIN + rows)]
    acc[...] = key_grads(middle).reshape(acc.shape)

    def totals(half):
        return (
            remote(ztot.at[0, half], zin.at[0, half], y_send.at[0, half], y_recv.at[0, half], left),
            remote(ztot.at[1, half], zin.at[1, half], y_send.at[1, half], y_recv.at[1, half], right),
        )

    def relays(half):
        return (
            remote(zin.at[0, half], zin.at[2, half], y_send.at[2, half], y_recv.at[2, half], left),
            remote(zin.at[1, half], zin.at[3, half], y_send.at[3, half], y_recv.at[3, half], right),
        )

    for half, back in ((0, back_down), (1, back_up)):
        back.wait_recv()
        for side in range(2):
            summed = acc[side, pl.ds(MARGIN * half, MARGIN)] + rmar[1 - half, side].astype(F32)
            ztot[side, half] = summed.astype(BF16)
        for copy in totals(half):
            copy.start()
    for half in range(2):
        for copy, relay in zip(totals(half), relays(half)):
            copy.wait_recv()
            relay.start()

    def gap_is(other, side, distance):
        other = lax.rem(other + 2 * views, views)
        gap = other - partners[other, 0] if side == 0 else partners[other, 1] - other
        return jnp.where(lax.rem(gap + views, views) == distance, 1, 0)

    use = (
        gap_is(cam + step, 0, step),
        gap_is(cam - step, 1, step),
        gap_is(cam + 2 * step, 0, 2 * step),
        gap_is(cam - 2 * step, 1, 2 * step),
    )
    for half in range(2):
        for copy in relays(half):
            copy.wait_recv()
        summed = own[pl.ds(MARGIN * half, MARGIN)]
        for source in range(4):
            summed = summed + jnp.where(use[source] > 0, zin[source, half].astype(F32), 0.0)
        gout[pl.ds(MARGIN * half, MARGIN)] = summed.astype(BF16)
    grad_copy = pltpu.make_async_copy(gout, grad_out.at[0], out_sem.at[1])
    grad_copy.start()

    halo_up.wait_send()
    halo_down.wait_send()
    for r in range(rows):
        for copy in (*near(r), *far(r)):
            copy.wait_send()
    for copy in margins:
        copy.wait_send()
    back_up.wait_send()
    back_down.wait_send()
    for half in range(2):
        for copy in (*totals(half), *relays(half)):
            copy.wait_send()
    att_copy.wait()
    grad_copy.wait()


def local(
    views,
    slabs,
    features_in,
    conv_weight,
    q_weight,
    k_weight,
    v_weight,
    partners,
    band_widths,
    bands,
    grad_attended,
):
    _, rows, width, channels = features_in.shape
    block = (width, channels)
    half = rows // 2
    hbm = pl.BlockSpec(memory_space=pl.ANY)
    smem = pl.BlockSpec(memory_space=pltpu.SMEM)
    dma = pltpu.SemaphoreType.DMA
    out = jax.ShapeDtypeStruct(features_in.shape, BF16)
    return pl.pallas_call(
        functools.partial(kernel, views, slabs),
        out_shape=(out, out),
        in_specs=[hbm, hbm, hbm, hbm, hbm, smem, smem, smem, hbm],
        out_specs=(hbm, hbm),
        scratch_shapes=[
            pltpu.VMEM((rows + 2, *block), BF16),
            pltpu.VMEM(conv_weight.shape, BF16),
            pltpu.VMEM(q_weight.shape, BF16),
            pltpu.VMEM(q_weight.shape, BF16),
            pltpu.VMEM(q_weight.shape, BF16),
            pltpu.VMEM((rows, *block), BF16),
            pltpu.VMEM((rows, *block), BF16),
            pltpu.VMEM((4, rows, *block), BF16),
            pltpu.VMEM((2, rows + 2 * MARGIN, *block), BF16),
            pltpu.VMEM((rows, 2 * width, channels), BF16),
            pltpu.VMEM((rows, 2 * BAND + 1, BLOCK, 2 * width), BF16),
            pltpu.VMEM((rows, *block), BF16),
            pltpu.VMEM((rows, *block), F32),
            pltpu.VMEM((2, rows, *block), F32),
            pltpu.VMEM((2, 2, MARGIN, *block), BF16),
            pltpu.VMEM((2, 2, MARGIN, *block), BF16),
            pltpu.VMEM((2, 2, half, *block), BF16),
            pltpu.VMEM((4, 2, half, *block), BF16),
            pltpu.VMEM((rows, *block), BF16),
            dma((6,)),
            dma((2,)),
            dma((2,)),
            dma((4, rows)),
            dma((4, rows)),
            dma((2, 2)),
            dma((2, 2)),
            dma((2,)),
            dma((2,)),
            dma((4, 2)),
            dma((4, 2)),
            dma((2,)),
        ],
        compiler_params=pltpu.CompilerParams(collective_id=0, has_side_effects=True),
        name="views",
    )(
        features_in,
        conv_weight,
        q_weight,
        k_weight,
        v_weight,
        partners,
        band_widths,
        bands,
        grad_attended,
    )


def solution(mesh):
    placed = (
        P("cam", "row", None, None),
        P(),
        P(),
        P(),
        P(),
        P(),
        P(),
        P("cam", "row", None, None),
        P("cam", "row", None, None),
    )
    return jax.shard_map(
        functools.partial(local, mesh.shape["cam"], mesh.shape["row"]),
        mesh=mesh,
        in_specs=placed,
        out_specs=(P("cam", "row", None, None), P("cam", "row", None, None)),
        check_vma=False,
    )
```

```python
import functools

import jax
import jax.numpy as jnp
from jax import lax
from jax.experimental import pallas as pl
from jax.experimental.pallas import tpu as pltpu
from jax.sharding import PartitionSpec as P

MESH = pl.DeviceIdType.MESH
BLOCK = 128
MARGIN = 2
BAND = 3
F32 = jnp.float32
BF16 = jnp.bfloat16

NN = (((1,), (0,)), ((), ()))
NT = (((1,), (1,)), ((), ()))
TN = (((0,), (0,)), ((), ()))


def dot(a, b, dims=NN):
    return lax.dot_general(a, b, dims, preferred_element_type=F32)


def kernel(
    views,
    slabs,
    feat,
    conv_w,
    q_w,
    k_w,
    v_w,
    partners,
    widths,
    bands,
    grad_att,
    att_out,
    grad_out,
    fbuf,
    wconv,
    wq,
    wk,
    wv,
    dabuf,
    hwin,
    cand,
    wsel,
    qa,
    pd,
    att,
    own,
    gmar,
    rmar,
    ztot,
    zin,
    gout,
    load_sem,
    halo_send,
    halo_recv,
    z_send,
    z_recv,
    m_send,
    m_recv,
    b_send,
    b_recv,
    y_send,
    y_recv,
    out_sem,
):
    step = views // min(16, views)
    rows = dabuf.shape[0]
    width, channels = dabuf.shape[1], dabuf.shape[2]
    reach = MARGIN + 1
    cam = lax.axis_index("cam")
    slab = lax.axis_index("row")
    cam_r, cam_l = lax.rem(cam + step, views), lax.rem(cam + views - step, views)
    odd = lax.rem(slab, 2)

    def by_core(even_value, odd_value):
        return even_value + (odd_value - even_value) * odd

    inner_slab = by_core(slab + 1, slab - 1)
    outer_slab = by_core(lax.rem(slab + slabs - 1, slabs), lax.rem(slab + 1, slabs))
    right, left = (cam_r, slab), (cam_l, slab)
    inner, outer = (cam, inner_slab), (cam, outer_slab)

    barrier = pltpu.get_barrier_semaphore()
    for peer in (outer, inner, right, left):
        pl.semaphore_signal(barrier, inc=1, device_id=peer, device_id_type=MESH)

    loads = [
        pltpu.make_async_copy(feat.at[0], fbuf.at[pl.ds(reach, rows)], load_sem.at[0]),
        pltpu.make_async_copy(conv_w, wconv, load_sem.at[1]),
        pltpu.make_async_copy(grad_att.at[0], dabuf, load_sem.at[2]),
        pltpu.make_async_copy(v_w, wv, load_sem.at[3]),
        pltpu.make_async_copy(q_w, wq, load_sem.at[4]),
        pltpu.make_async_copy(k_w, wk, load_sem.at[5]),
    ]
    for load in loads:
        load.start()

    def remote(src, dst, send, recv, peer):
        return pltpu.make_async_remote_copy(
            src_ref=src, dst_ref=dst, send_sem=send, recv_sem=recv, device_id=peer, device_id_type=MESH
        )

    halo_outer = remote(
        feat.at[0, pl.ds(by_core(0, rows - reach), reach)],
        fbuf.at[pl.ds(by_core(rows + reach, 0), reach)],
        halo_send.at[0],
        halo_recv.at[0],
        outer,
    )
    halo_inner = remote(
        feat.at[0, by_core(rows - 1, 0)],
        fbuf.at[by_core(reach - 1, rows + reach)],
        halo_send.at[1],
        halo_recv.at[1],
        inner,
    )
    edge_row = by_core(MARGIN + rows - 1, MARGIN)
    far_rows = by_core(0, MARGIN + rows - 1)
    places = [*range(MARGIN + 1, MARGIN + rows - 1), edge_row, *[far_rows + k for k in range(reach)]]
    n_inner = rows - 1

    def near(k):
        r = places[k]
        return (
            remote(hwin.at[r], cand.at[0, r], z_send.at[0, k], z_recv.at[0, k], right),
            remote(hwin.at[r], cand.at[2, r], z_send.at[2, k], z_recv.at[2, k], left),
        )

    def far(k):
        r = places[k]
        return (
            remote(cand.at[0, r], cand.at[1, r], z_send.at[1, k], z_recv.at[1, k], right),
            remote(cand.at[2, r], cand.at[3, r], z_send.at[3, k], z_recv.at[3, k], left),
        )

    def conv(start, count):
        total = None
        for dy in range(3):
            weight = jnp.concatenate([wconv[dy, 0], wconv[dy, 1], wconv[dy, 2]], axis=1)
            tap = fbuf[pl.ds(start + dy, count)].reshape(count * width, channels)
            part = dot(tap, weight)
            total = part if total is None else total + part
        size = count * width
        pixel = lax.rem(lax.broadcasted_iota(jnp.int32, (size, channels), 0), width)
        before = pltpu.roll(total[:, :channels], 1, 0)
        after = pltpu.roll(total[:, 2 * channels :], size - 1, 0)
        out = total[:, channels : 2 * channels]
        out = out + jnp.where(pixel == 0, 0.0, before) + jnp.where(pixel == width - 1, 0.0, after)
        hwin[pl.ds(start, count)] = out.astype(BF16).reshape(count, width, channels)

    def relay(ks):
        for k in ks:
            for near_copy, far_copy in zip(near(k), far(k)):
                near_copy.wait_recv()
                far_copy.start()

    def launch(ks):
        for k in ks:
            for copy in near(k):
                copy.start()

    pl.semaphore_wait(barrier, 4)
    halo_outer.start()
    halo_inner.start()
    loads[0].wait()
    loads[1].wait()
    conv(MARGIN + 1, rows - 2)
    launch(range(rows - 2))

    loads[2].wait()
    loads[3].wait()
    loads[4].wait()
    loads[5].wait()
    grad_v = dot(dabuf[...].reshape(rows * width, channels), wv[...], NT).astype(BF16)
    qa[:, pl.ds(width, width), :] = grad_v.reshape(rows, width, channels)
    pd[:, 2 * BAND] = jnp.zeros((rows, BLOCK, 2 * width), BF16)

    halo_inner.wait_recv()
    conv(edge_row, 1)
    launch([rows - 2])
    relay(range(n_inner))

    halo_outer.wait_recv()

    @pl.when(jnp.logical_or(slab == 0, slab == slabs - 1))
    def _():
        fbuf[pl.ds(by_core(0, rows + reach), reach)] = jnp.zeros((reach, width, channels), BF16)

    conv(far_rows, reach)
    launch(range(n_inner, n_inner + reach))

    scale = channels**-0.5
    queries = dot(hwin[pl.ds(MARGIN, rows)].reshape(rows * width, channels), wq[...]).astype(BF16)
    queries = (dot(queries, wk[...], NT) * scale).astype(BF16)
    qa[:, pl.ds(0, width), :] = queries.reshape(rows, width, channels)

    gap0 = lax.rem(cam - partners[0, cam] + views, views)
    gap1 = lax.rem(partners[1, cam] - cam + views, views)

    def select(ks):
        for k in ks:
            r = places[k]
            for copy in far(k):
                copy.wait_recv()
            wsel[0, r] = jnp.where(gap0 == step, cand[0, r], cand[1, r])
            wsel[1, r] = jnp.where(gap1 == step, cand[2, r], cand[3, r])

    relay(range(n_inner, n_inner + reach))
    select(range(n_inner))
    mine = pl.ds(by_core(rows, MARGIN), MARGIN)
    theirs = pl.ds(by_core(0, MARGIN + rows), MARGIN)
    margins = [
        remote(wsel.at[side, mine], wsel.at[side, theirs], m_send.at[side], m_recv.at[side], inner)
        for side in range(2)
    ]
    for copy in margins:
        copy.start()
    select(range(n_inner, n_inner + reach))
    for copy in margins:
        copy.wait_recv()

    base = slab * rows - MARGIN

    def attend(q, carry):
        qa_here = qa[q]
        keys, exps, grads = [], [], []
        total, weighted = None, None
        for side in range(2):
            for slot in range(BAND):
                place = jnp.clip(bands[0, slot, side, q] - base, 0, rows + 2 * MARGIN - 1)
                block = wsel[side, place]
                both = dot(block, qa_here, NT)
                live = jnp.where(slot < widths[side, cam], 1.0, 0.0).astype(F32)
                expo = jnp.where(live > 0.0, jnp.exp(both[:, :width]), 0.0)
                grad = both[:, width:]
                keys.append(block)
                exps.append(expo)
                grads.append(grad)
                here = jnp.sum(expo, axis=0, keepdims=True)
                here_w = jnp.sum(expo * grad, axis=0, keepdims=True)
                total = here if total is None else total + here
                weighted = here_w if weighted is None else weighted + here_w
        inverse = 1.0 / total
        delta = weighted * inverse
        pairs = []
        for place in range(2 * BAND):
            prob = exps[place] * inverse
            score = prob * (grads[place] - delta)
            pair = jnp.concatenate([score.astype(BF16), prob.astype(BF16)], axis=1)
            pd[q, place] = pair
            pairs.append(pair)
        mixed = dot(jnp.concatenate(keys, axis=0), jnp.concatenate(pairs, axis=0), TN).astype(BF16)
        att[q] = dot(mixed[:, width:], wv[...], TN).astype(BF16)
        grad_q = (dot(mixed[:, :width], wk[...], TN) * scale).astype(BF16)
        own[q] = dot(grad_q, wq[...], NT)
        return carry

    lax.fori_loop(0, rows, attend, 0)

    att_copy = pltpu.make_async_copy(att, att_out.at[0], out_sem.at[0])
    att_copy.start()

    def place_of(q, side, row):
        place = jnp.int32(2 * BAND)
        for slot in range(BAND):
            place = jnp.where(bands[0, slot, side, q] - base == row, side * BAND + slot, place)
        return place

    def key_grads(first):
        summed = None
        for q in range(rows):
            lhs = jnp.concatenate(
                [pd[q, place_of(q, side, first + i)] for side in range(2) for i in range(MARGIN)], axis=0
            )
            part = dot(lhs, qa[q])
            summed = part if summed is None else summed + part
        return summed.reshape(2, MARGIN, BLOCK, channels)

    gmar[1] = key_grads(by_core(0, MARGIN + rows)).astype(BF16)
    back = [
        remote(gmar.at[0], rmar.at[0], b_send.at[0], b_recv.at[0], inner),
        remote(gmar.at[1], rmar.at[1], b_send.at[1], b_recv.at[1], outer),
    ]
    back[1].start()
    gmar[0] = key_grads(by_core(MARGIN + rows, 0)).astype(BF16)
    back[0].start()

    def totals(half):
        return (
            remote(ztot.at[0, half], zin.at[0, half], y_send.at[0, half], y_recv.at[0, half], left),
            remote(ztot.at[1, half], zin.at[1, half], y_send.at[1, half], y_recv.at[1, half], right),
        )

    def relays(half):
        return (
            remote(zin.at[0, half], zin.at[2, half], y_send.at[2, half], y_recv.at[2, half], left),
            remote(zin.at[1, half], zin.at[3, half], y_send.at[3, half], y_recv.at[3, half], right),
        )

    firsts = (by_core(MARGIN, 0), by_core(0, MARGIN))

    def send_half(half):
        summed = key_grads(MARGIN + firsts[half])
        back[half].wait_recv()
        ztot[:, half] = (summed + rmar[half].astype(F32)).astype(BF16)
        for copy in totals(half):
            copy.start()

    def relay_half(half):
        for copy, onward in zip(totals(half), relays(half)):
            copy.wait_recv()
            onward.start()

    send_half(0)
    send_half(1)
    relay_half(0)
    relay_half(1)

    def gap_is(other, side, distance):
        other = lax.rem(other + 2 * views, views)
        gap = other - partners[0, other] if side == 0 else partners[1, other] - other
        return jnp.where(lax.rem(gap + views, views) == distance, 1, 0)

    use = (
        gap_is(cam + step, 0, step),
        gap_is(cam - step, 1, step),
        gap_is(cam + 2 * step, 0, 2 * step),
        gap_is(cam - 2 * step, 1, 2 * step),
    )
    for half in range(2):
        for copy in relays(half):
            copy.wait_recv()
        summed = own[pl.ds(firsts[half], MARGIN)]
        for source in range(4):
            summed = summed + jnp.where(use[source] > 0, zin[source, half].astype(F32), 0.0)
        gout[pl.ds(firsts[half], MARGIN)] = summed.astype(BF16)
    grad_copy = pltpu.make_async_copy(gout, grad_out.at[0], out_sem.at[1])
    grad_copy.start()

    halo_outer.wait_send()
    halo_inner.wait_send()
    for k in range(n_inner + reach):
        for copy in (*near(k), *far(k)):
            copy.wait_send()
    for copy in (*margins, *back):
        copy.wait_send()
    for half in range(2):
        for copy in (*totals(half), *relays(half)):
            copy.wait_send()
    att_copy.wait()
    grad_copy.wait()


def local(
    views,
    slabs,
    features_in,
    conv_weight,
    q_weight,
    k_weight,
    v_weight,
    partners,
    band_widths,
    bands,
    grad_attended,
):
    _, rows, width, channels = features_in.shape
    block = (width, channels)
    chunks = rows + MARGIN
    hbm = pl.BlockSpec(memory_space=pl.ANY)
    smem = pl.BlockSpec(memory_space=pltpu.SMEM)
    dma = pltpu.SemaphoreType.DMA
    out = jax.ShapeDtypeStruct(features_in.shape, BF16)
    return pl.pallas_call(
        functools.partial(kernel, views, slabs),
        out_shape=(out, out),
        in_specs=[hbm, hbm, hbm, hbm, hbm, smem, smem, smem, hbm],
        out_specs=(hbm, hbm),
        scratch_shapes=[
            pltpu.VMEM((rows + 2 * MARGIN + 2, *block), BF16),
            pltpu.VMEM(conv_weight.shape, BF16),
            pltpu.VMEM(q_weight.shape, BF16),
            pltpu.VMEM(q_weight.shape, BF16),
            pltpu.VMEM(q_weight.shape, BF16),
            pltpu.VMEM((rows, *block), BF16),
            pltpu.VMEM((rows + 2 * MARGIN, *block), BF16),
            pltpu.VMEM((4, rows + 2 * MARGIN, *block), BF16),
            pltpu.VMEM((2, rows + 2 * MARGIN, *block), BF16),
            pltpu.VMEM((rows, 2 * width, channels), BF16),
            pltpu.VMEM((rows, 2 * BAND + 1, BLOCK, 2 * width), BF16),
            pltpu.VMEM((rows, *block), BF16),
            pltpu.VMEM((rows, *block), F32),
            pltpu.VMEM((2, 2, MARGIN, *block), BF16),
            pltpu.VMEM((2, 2, MARGIN, *block), BF16),
            pltpu.VMEM((2, 2, MARGIN, *block), BF16),
            pltpu.VMEM((4, 2, MARGIN, *block), BF16),
            pltpu.VMEM((rows, *block), BF16),
            dma((6,)),
            dma((2,)),
            dma((2,)),
            dma((4, chunks)),
            dma((4, chunks)),
            dma((2,)),
            dma((2,)),
            dma((2,)),
            dma((2,)),
            dma((4, 2)),
            dma((4, 2)),
            dma((2,)),
        ],
        compiler_params=pltpu.CompilerParams(collective_id=0, has_side_effects=True),
        name="views",
    )(
        features_in,
        conv_weight,
        q_weight,
        k_weight,
        v_weight,
        partners.T,
        band_widths.T,
        bands.transpose(0, 3, 2, 1),
        grad_attended,
    )


def solution(mesh):
    placed = (
        P("cam", "row", None, None),
        P(),
        P(),
        P(),
        P(),
        P(),
        P(),
        P("cam", "row", None, None),
        P("cam", "row", None, None),
    )
    return jax.shard_map(
        functools.partial(local, mesh.shape["cam"], mesh.shape["row"]),
        mesh=mesh,
        in_specs=placed,
        out_specs=(P("cam", "row", None, None), P("cam", "row", None, None)),
        check_vma=False,
    )
```

```python
import functools

import jax
import jax.numpy as jnp
from jax import lax
from jax.experimental import pallas as pl
from jax.experimental.pallas import tpu as pltpu
from jax.sharding import PartitionSpec as P

MESH = pl.DeviceIdType.MESH
BLOCK = 128
MARGIN = 2
BAND = 3
F32 = jnp.float32
BF16 = jnp.bfloat16

NN = (((1,), (0,)), ((), ()))
NT = (((1,), (1,)), ((), ()))
TN = (((0,), (0,)), ((), ()))


def dot(a, b, dims=NN):
    return lax.dot_general(a, b, dims, preferred_element_type=F32)


def kernel(
    views,
    slabs,
    feat,
    conv_w,
    q_w,
    k_w,
    v_w,
    partners,
    widths,
    bands,
    grad_att,
    att_out,
    grad_out,
    fbuf,
    wconv,
    wq,
    wk,
    wv,
    dabuf,
    hwin,
    cand,
    wsel,
    qa,
    pd,
    own,
    gmar,
    rmar,
    ztot,
    zin,
    load_sem,
    halo_send,
    halo_recv,
    z_send,
    z_recv,
    m_send,
    m_recv,
    b_send,
    b_recv,
    y_send,
    y_recv,
):
    step = views // min(16, views)
    rows = dabuf.shape[0]
    width, channels = dabuf.shape[1], dabuf.shape[2]
    reach = MARGIN + 1
    cam = lax.axis_index("cam")
    slab = lax.axis_index("row")
    cam_r, cam_l = lax.rem(cam + step, views), lax.rem(cam + views - step, views)
    odd = lax.rem(slab, 2)

    def by_core(even_value, odd_value):
        return even_value + (odd_value - even_value) * odd

    inner_slab = by_core(slab + 1, slab - 1)
    outer_slab = by_core(lax.rem(slab + slabs - 1, slabs), lax.rem(slab + 1, slabs))
    right, left = (cam_r, slab), (cam_l, slab)
    inner, outer = (cam, inner_slab), (cam, outer_slab)

    barrier = pltpu.get_barrier_semaphore()
    for peer in (outer, inner, right, left):
        pl.semaphore_signal(barrier, inc=1, device_id=peer, device_id_type=MESH)

    loads = [
        pltpu.make_async_copy(feat.at[0], fbuf.at[pl.ds(reach, rows)], load_sem.at[0]),
        pltpu.make_async_copy(conv_w, wconv, load_sem.at[1]),
        pltpu.make_async_copy(grad_att.at[0], dabuf, load_sem.at[2]),
        pltpu.make_async_copy(v_w, wv, load_sem.at[3]),
        pltpu.make_async_copy(q_w, wq, load_sem.at[4]),
        pltpu.make_async_copy(k_w, wk, load_sem.at[5]),
    ]
    for load in loads:
        load.start()

    def remote(src, dst, send, recv, peer):
        return pltpu.make_async_remote_copy(
            src_ref=src, dst_ref=dst, send_sem=send, recv_sem=recv, device_id=peer, device_id_type=MESH
        )

    halo_outer = remote(
        feat.at[0, pl.ds(by_core(0, rows - reach), reach)],
        fbuf.at[pl.ds(by_core(rows + reach, 0), reach)],
        halo_send.at[0],
        halo_recv.at[0],
        outer,
    )
    halo_inner = remote(
        feat.at[0, by_core(rows - 1, 0)],
        fbuf.at[by_core(reach - 1, rows + reach)],
        halo_send.at[1],
        halo_recv.at[1],
        inner,
    )
    edge_row = by_core(MARGIN + rows - 1, MARGIN)
    far_rows = by_core(0, MARGIN + rows - 1)
    places = [*range(MARGIN + 1, MARGIN + rows - 1), edge_row, *[far_rows + k for k in range(reach)]]
    n_inner = rows - 1

    def near(k):
        r = places[k]
        return (
            remote(hwin.at[r], cand.at[0, r], z_send.at[0, k], z_recv.at[0, k], right),
            remote(hwin.at[r], cand.at[2, r], z_send.at[2, k], z_recv.at[2, k], left),
        )

    def far(k):
        r = places[k]
        return (
            remote(cand.at[0, r], cand.at[1, r], z_send.at[1, k], z_recv.at[1, k], right),
            remote(cand.at[2, r], cand.at[3, r], z_send.at[3, k], z_recv.at[3, k], left),
        )

    def conv(start, count):
        total = None
        for dy in range(3):
            weight = jnp.concatenate([wconv[dy, 0], wconv[dy, 1], wconv[dy, 2]], axis=1)
            tap = fbuf[pl.ds(start + dy, count)].reshape(count * width, channels)
            part = dot(tap, weight)
            total = part if total is None else total + part
        size = count * width
        pixel = lax.rem(lax.broadcasted_iota(jnp.int32, (size, channels), 0), width)
        before = pltpu.roll(total[:, :channels], 1, 0)
        after = pltpu.roll(total[:, 2 * channels :], size - 1, 0)
        out = total[:, channels : 2 * channels]
        out = out + jnp.where(pixel == 0, 0.0, before) + jnp.where(pixel == width - 1, 0.0, after)
        hwin[pl.ds(start, count)] = out.astype(BF16).reshape(count, width, channels)

    def relay(ks):
        for k in ks:
            for near_copy, far_copy in zip(near(k), far(k)):
                near_copy.wait_recv()
                far_copy.start()

    def launch(ks):
        for k in ks:
            for copy in near(k):
                copy.start()

    pl.semaphore_wait(barrier, 4)
    halo_outer.start()
    halo_inner.start()
    loads[0].wait()
    loads[1].wait()
    conv(MARGIN + 1, rows - 2)
    launch(range(rows - 2))

    loads[2].wait()
    loads[3].wait()
    loads[4].wait()
    loads[5].wait()
    grad_v = dot(dabuf[...].reshape(rows * width, channels), wv[...], NT).astype(BF16)
    qa[:, pl.ds(width, width), :] = grad_v.reshape(rows, width, channels)
    pd[:, 2 * BAND] = jnp.zeros((rows, BLOCK, 2 * width), BF16)

    halo_inner.wait_recv()
    conv(edge_row, 1)
    launch([rows - 2])
    relay(range(rows - 2))
    halo_outer.wait_recv()

    @pl.when(jnp.logical_or(slab == 0, slab == slabs - 1))
    def _():
        fbuf[pl.ds(by_core(0, rows + reach), reach)] = jnp.zeros((reach, width, channels), BF16)

    conv(far_rows, reach)
    launch(range(n_inner, n_inner + reach))
    relay([rows - 2])

    scale = channels**-0.5
    queries = dot(hwin[pl.ds(MARGIN, rows)].reshape(rows * width, channels), wq[...]).astype(BF16)
    queries = (dot(queries, wk[...], NT) * scale).astype(BF16)
    qa[:, pl.ds(0, width), :] = queries.reshape(rows, width, channels)

    gap0 = lax.rem(cam - partners[0, cam] + views, views)
    gap1 = lax.rem(partners[1, cam] - cam + views, views)

    def select(ks):
        for k in ks:
            r = places[k]
            for copy in far(k):
                copy.wait_recv()
            wsel[0, r] = jnp.where(gap0 == step, cand[0, r], cand[1, r])
            wsel[1, r] = jnp.where(gap1 == step, cand[2, r], cand[3, r])

    relay(range(n_inner, n_inner + reach))
    select(range(n_inner))
    mine = pl.ds(by_core(rows, MARGIN), MARGIN)
    theirs = pl.ds(by_core(0, MARGIN + rows), MARGIN)
    margins = [
        remote(wsel.at[side, mine], wsel.at[side, theirs], m_send.at[side], m_recv.at[side], inner)
        for side in range(2)
    ]
    for copy in margins:
        copy.start()
    select(range(n_inner, n_inner + reach))
    for copy in margins:
        copy.wait_recv()

    base = slab * rows - MARGIN

    def key_block(q, side, slot):
        return wsel[side, jnp.clip(bands[0, slot, side, q] - base, 0, rows + 2 * MARGIN - 1)]

    lists = [(side, slot) for side in range(2) for slot in range(BAND)]

    def attend(q):
        qa_here = qa[q]
        exps, grads = [], []
        total, weighted = None, None
        for side, slot in lists:
            both = dot(key_block(q, side, slot), qa_here, NT)
            expo = jnp.where(slot < widths[side, cam], jnp.exp(both[:, :width]), 0.0)
            grad = both[:, width:]
            exps.append(expo)
            grads.append(grad)
            here = jnp.sum(expo, axis=0, keepdims=True)
            here_w = jnp.sum(expo * grad, axis=0, keepdims=True)
            total = here if total is None else total + here
            weighted = here_w if weighted is None else weighted + here_w
        inverse = 1.0 / total
        delta = weighted * inverse
        for place in range(2 * BAND):
            prob = exps[place] * inverse
            score = prob * (grads[place] - delta)
            pd[q, place] = jnp.concatenate([score.astype(BF16), prob.astype(BF16)], axis=1)

    def combine(q):
        keys = jnp.concatenate([key_block(q, side, slot) for side, slot in lists], axis=0)
        pairs = pd[q, pl.ds(0, 2 * BAND)].reshape(2 * BAND * BLOCK, 2 * width)
        mixed = dot(keys, pairs, TN).astype(BF16)
        att_out[0, q] = dot(mixed[:, width:], wv[...], TN).astype(BF16)
        grad_q = (dot(mixed[:, :width], wk[...], TN) * scale).astype(BF16)
        own[q] = dot(grad_q, wq[...], NT)

    for q in range(rows):
        attend(q)

    def place_of(q, side, row):
        place = jnp.int32(2 * BAND)
        for slot in range(BAND):
            place = jnp.where(bands[0, slot, side, q] - base == row, side * BAND + slot, place)
        return place

    def key_grads(first):
        summed = None
        for q in range(rows):
            lhs = jnp.concatenate(
                [pd[q, place_of(q, side, first + i)] for side in range(2) for i in range(MARGIN)], axis=0
            )
            part = dot(lhs, qa[q])
            summed = part if summed is None else summed + part
        return summed.reshape(2, MARGIN, BLOCK, channels)

    gmar[1] = key_grads(by_core(0, MARGIN + rows)).astype(BF16)
    back = [
        remote(gmar.at[0], rmar.at[0], b_send.at[0], b_recv.at[0], inner),
        remote(gmar.at[1], rmar.at[1], b_send.at[1], b_recv.at[1], outer),
    ]
    back[1].start()
    gmar[0] = key_grads(by_core(MARGIN + rows, 0)).astype(BF16)
    back[0].start()

    def totals(half, i):
        k = half * MARGIN + i
        return (
            remote(ztot.at[0, k], zin.at[0, k], y_send.at[0, k], y_recv.at[0, k], left),
            remote(ztot.at[1, k], zin.at[1, k], y_send.at[1, k], y_recv.at[1, k], right),
        )

    def relays(half, i):
        k = half * MARGIN + i
        return (
            remote(zin.at[0, k], zin.at[2, k], y_send.at[2, k], y_recv.at[2, k], left),
            remote(zin.at[1, k], zin.at[3, k], y_send.at[3, k], y_recv.at[3, k], right),
        )

    firsts = (by_core(MARGIN, 0), by_core(0, MARGIN))

    def send_half(half, summed):
        back[half].wait_recv()
        for i in range(MARGIN):
            for side in range(2):
                ztot[side, half * MARGIN + i] = (summed[side, i] + rmar[half, side, i].astype(F32)).astype(BF16)
            for copy in totals(half, i):
                copy.start()

    def relay_half(half):
        for i in range(MARGIN):
            for copy, onward in zip(totals(half, i), relays(half, i)):
                copy.wait_recv()
                onward.start()

    send_half(0, key_grads(MARGIN + firsts[0]))
    last_half = key_grads(MARGIN + firsts[1])
    for q in range(rows):
        combine(q)
    send_half(1, last_half)
    relay_half(0)
    relay_half(1)

    def gap_is(other, side, distance):
        other = lax.rem(other + 2 * views, views)
        gap = other - partners[0, other] if side == 0 else partners[1, other] - other
        return jnp.where(lax.rem(gap + views, views) == distance, 1, 0)

    use = (
        gap_is(cam + step, 0, step),
        gap_is(cam - step, 1, step),
        gap_is(cam + 2 * step, 0, 2 * step),
        gap_is(cam - 2 * step, 1, 2 * step),
    )
    for half in range(2):
        for i in range(MARGIN):
            for copy in relays(half, i):
                copy.wait_recv()
            summed = own[firsts[half] + i]
            for source in range(4):
                summed = summed + jnp.where(use[source] > 0, zin[source, half * MARGIN + i].astype(F32), 0.0)
            grad_out[0, firsts[half] + i] = summed.astype(BF16)

    halo_outer.wait_send()
    halo_inner.wait_send()
    for k in range(n_inner + reach):
        for copy in (*near(k), *far(k)):
            copy.wait_send()
    for copy in (*margins, *back):
        copy.wait_send()
    for half in range(2):
        for i in range(MARGIN):
            for copy in (*totals(half, i), *relays(half, i)):
                copy.wait_send()


def local(
    views,
    slabs,
    features_in,
    conv_weight,
    q_weight,
    k_weight,
    v_weight,
    partners,
    band_widths,
    bands,
    grad_attended,
):
    _, rows, width, channels = features_in.shape
    block = (width, channels)
    chunks = rows + MARGIN
    hbm = pl.BlockSpec(memory_space=pl.ANY)
    vmem = pl.BlockSpec(memory_space=pltpu.VMEM)
    smem = pl.BlockSpec(memory_space=pltpu.SMEM)
    dma = pltpu.SemaphoreType.DMA
    out = jax.ShapeDtypeStruct(features_in.shape, BF16)
    return pl.pallas_call(
        functools.partial(kernel, views, slabs),
        out_shape=(out, out),
        in_specs=[hbm, hbm, hbm, hbm, hbm, smem, smem, smem, hbm],
        out_specs=(vmem, vmem),
        scratch_shapes=[
            pltpu.VMEM((rows + 2 * MARGIN + 2, *block), BF16),
            pltpu.VMEM(conv_weight.shape, BF16),
            pltpu.VMEM(q_weight.shape, BF16),
            pltpu.VMEM(q_weight.shape, BF16),
            pltpu.VMEM(q_weight.shape, BF16),
            pltpu.VMEM((rows, *block), BF16),
            pltpu.VMEM((rows + 2 * MARGIN, *block), BF16),
            pltpu.VMEM((4, rows + 2 * MARGIN, *block), BF16),
            pltpu.VMEM((2, rows + 2 * MARGIN, *block), BF16),
            pltpu.VMEM((rows, 2 * width, channels), BF16),
            pltpu.VMEM((rows, 2 * BAND + 1, BLOCK, 2 * width), BF16),
            pltpu.VMEM((rows, *block), F32),
            pltpu.VMEM((2, 2, MARGIN, *block), BF16),
            pltpu.VMEM((2, 2, MARGIN, *block), BF16),
            pltpu.VMEM((2, rows, *block), BF16),
            pltpu.VMEM((4, rows, *block), BF16),
            dma((6,)),
            dma((2,)),
            dma((2,)),
            dma((4, chunks)),
            dma((4, chunks)),
            dma((2,)),
            dma((2,)),
            dma((2,)),
            dma((2,)),
            dma((4, rows)),
            dma((4, rows)),
        ],
        compiler_params=pltpu.CompilerParams(collective_id=0, has_side_effects=True),
        name="views",
    )(
        features_in,
        conv_weight,
        q_weight,
        k_weight,
        v_weight,
        partners.T,
        band_widths.T,
        bands.transpose(0, 3, 2, 1),
        grad_attended,
    )


def solution(mesh):
    placed = (
        P("cam", "row", None, None),
        P(),
        P(),
        P(),
        P(),
        P(),
        P(),
        P("cam", "row", None, None),
        P("cam", "row", None, None),
    )
    return jax.shard_map(
        functools.partial(local, mesh.shape["cam"], mesh.shape["row"]),
        mesh=mesh,
        in_specs=placed,
        out_specs=(P("cam", "row", None, None), P("cam", "row", None, None)),
        check_vma=False,
    )
```

```python
import functools

import jax
import jax.numpy as jnp
from jax import lax
from jax.experimental import pallas as pl
from jax.experimental.pallas import tpu as pltpu
from jax.sharding import PartitionSpec as P

MESH = pl.DeviceIdType.MESH
BLOCK = 128
MARGIN = 2
BAND = 3
F32 = jnp.float32
BF16 = jnp.bfloat16

NN = (((1,), (0,)), ((), ()))
NT = (((1,), (1,)), ((), ()))
TN = (((0,), (0,)), ((), ()))


def dot(a, b, dims=NN):
    return lax.dot_general(a, b, dims, preferred_element_type=F32)


def kernel(
    views,
    slabs,
    feat,
    conv_w,
    q_w,
    k_w,
    v_w,
    partners_in,
    widths_in,
    bands_in,
    grad_att,
    att_out,
    grad_out,
    partners,
    widths,
    bands,
    fbuf,
    wconv,
    wq,
    wk,
    wv,
    dabuf,
    hwin,
    cand,
    wsel,
    qa,
    pd,
    own,
    gmar,
    rmar,
    ztot,
    zin,
    att,
    gout,
    load_sem,
    halo_send,
    halo_recv,
    z_send,
    z_recv,
    m_send,
    m_recv,
    b_send,
    b_recv,
    y_send,
    y_recv,
    out_sem,
):
    step = views // min(16, views)
    rows = dabuf.shape[0]
    width, channels = dabuf.shape[1], dabuf.shape[2]
    reach = MARGIN + 1
    cam = lax.axis_index("cam")
    slab = lax.axis_index("row")
    cam_r, cam_l = lax.rem(cam + step, views), lax.rem(cam + views - step, views)
    odd = lax.rem(slab, 2)

    def by_core(even_value, odd_value):
        return even_value + (odd_value - even_value) * odd

    inner_slab = by_core(slab + 1, slab - 1)
    outer_slab = by_core(lax.rem(slab + slabs - 1, slabs), lax.rem(slab + 1, slabs))
    right, left = (cam_r, slab), (cam_l, slab)
    inner, outer = (cam, inner_slab), (cam, outer_slab)

    barrier = pltpu.get_barrier_semaphore()
    for peer in (outer, inner, right, left):
        pl.semaphore_signal(barrier, inc=1, device_id=peer, device_id_type=MESH)

    loads = [
        pltpu.make_async_copy(feat.at[0], fbuf.at[pl.ds(reach, rows)], load_sem.at[0]),
        pltpu.make_async_copy(conv_w, wconv, load_sem.at[1]),
        pltpu.make_async_copy(grad_att.at[0], dabuf, load_sem.at[2]),
        pltpu.make_async_copy(v_w, wv, load_sem.at[3]),
        pltpu.make_async_copy(q_w, wq, load_sem.at[4]),
        pltpu.make_async_copy(k_w, wk, load_sem.at[5]),
        pltpu.make_async_copy(partners_in, partners, load_sem.at[6]),
        pltpu.make_async_copy(widths_in, widths, load_sem.at[7]),
        pltpu.make_async_copy(bands_in, bands, load_sem.at[8]),
    ]
    for load in loads:
        load.start()

    def remote(src, dst, send, recv, peer):
        return pltpu.make_async_remote_copy(
            src_ref=src, dst_ref=dst, send_sem=send, recv_sem=recv, device_id=peer, device_id_type=MESH
        )

    halo_outer = [
        remote(
            feat.at[0, by_core(0, rows - 1)],
            fbuf.at[by_core(rows + reach, reach - 1)],
            halo_send.at[0],
            halo_recv.at[0],
            outer,
        ),
        remote(
            feat.at[0, pl.ds(by_core(1, rows - reach), MARGIN)],
            fbuf.at[pl.ds(by_core(rows + reach + 1, 0), MARGIN)],
            halo_send.at[2],
            halo_recv.at[2],
            outer,
        ),
    ]
    halo_inner = remote(
        feat.at[0, by_core(rows - 1, 0)],
        fbuf.at[by_core(reach - 1, rows + reach)],
        halo_send.at[1],
        halo_recv.at[1],
        inner,
    )
    edge_row = by_core(MARGIN + rows - 1, MARGIN)
    outer_row = by_core(MARGIN, MARGIN + rows - 1)
    far_rows = by_core(0, MARGIN + rows)
    places = [*range(MARGIN + 1, MARGIN + rows - 1), edge_row, outer_row, *[far_rows + k for k in range(MARGIN)]]
    n_inner = rows - 1

    def near(k):
        r = places[k]
        return (
            remote(hwin.at[r], cand.at[0, r], z_send.at[0, k], z_recv.at[0, k], right),
            remote(hwin.at[r], cand.at[2, r], z_send.at[2, k], z_recv.at[2, k], left),
        )

    def far(k):
        r = places[k]
        return (
            remote(cand.at[0, r], cand.at[1, r], z_send.at[1, k], z_recv.at[1, k], right),
            remote(cand.at[2, r], cand.at[3, r], z_send.at[3, k], z_recv.at[3, k], left),
        )

    def conv(start, count):
        total = None
        for dy in range(3):
            weight = jnp.concatenate([wconv[dy, 0], wconv[dy, 1], wconv[dy, 2]], axis=1)
            tap = fbuf[pl.ds(start + dy, count)].reshape(count * width, channels)
            part = dot(tap, weight)
            total = part if total is None else total + part
        size = count * width
        pixel = lax.rem(lax.broadcasted_iota(jnp.int32, (size, channels), 0), width)
        before = pltpu.roll(total[:, :channels], 1, 0)
        after = pltpu.roll(total[:, 2 * channels :], size - 1, 0)
        out = total[:, channels : 2 * channels]
        out = out + jnp.where(pixel == 0, 0.0, before) + jnp.where(pixel == width - 1, 0.0, after)
        hwin[pl.ds(start, count)] = out.astype(BF16).reshape(count, width, channels)

    def relay(ks):
        for k in ks:
            for near_copy, far_copy in zip(near(k), far(k)):
                near_copy.wait_recv()
                far_copy.start()

    def launch(ks):
        for k in ks:
            for copy in near(k):
                copy.start()

    loads[0].wait()
    loads[1].wait()
    conv(MARGIN + 1, rows - 2)
    pl.semaphore_wait(barrier, 4)
    halo_outer[0].start()
    halo_inner.start()
    halo_outer[1].start()
    launch(range(rows - 2))

    loads[2].wait()
    loads[3].wait()
    loads[4].wait()
    loads[5].wait()
    grad_v = dot(dabuf[...].reshape(rows * width, channels), wv[...], NT).astype(BF16)
    qa[:, pl.ds(width, width), :] = grad_v.reshape(rows, width, channels)
    pd[:, 2 * BAND] = jnp.zeros((rows, BLOCK, 2 * width), BF16)

    halo_inner.wait_recv()
    conv(edge_row, 1)
    launch([rows - 2])
    relay([0])
    halo_outer[0].wait_recv()

    @pl.when(jnp.logical_or(slab == 0, slab == slabs - 1))
    def _():
        fbuf[by_core(reach - 1, rows + reach)] = jnp.zeros((width, channels), BF16)

    conv(outer_row, 1)
    launch([n_inner])
    halo_outer[1].wait_recv()
    conv(far_rows, MARGIN)
    launch(range(n_inner + 1, n_inner + reach))
    relay(range(1, n_inner))

    scale = channels**-0.5
    queries = dot(hwin[pl.ds(MARGIN, rows)].reshape(rows * width, channels), wq[...]).astype(BF16)
    queries = (dot(queries, wk[...], NT) * scale).astype(BF16)
    qa[:, pl.ds(0, width), :] = queries.reshape(rows, width, channels)

    for load in loads[6:]:
        load.wait()
    gap0 = lax.rem(cam - partners[0, cam] + views, views)
    gap1 = lax.rem(partners[1, cam] - cam + views, views)

    def select(ks):
        for k in ks:
            r = places[k]
            for copy in far(k):
                copy.wait_recv()
            wsel[0, r] = jnp.where(gap0 == step, cand[0, r], cand[1, r])
            wsel[1, r] = jnp.where(gap1 == step, cand[2, r], cand[3, r])

    relay(range(n_inner, n_inner + reach))
    select(range(n_inner))
    mine = pl.ds(by_core(rows, MARGIN), MARGIN)
    theirs = pl.ds(by_core(0, MARGIN + rows), MARGIN)
    margins = [
        remote(wsel.at[side, mine], wsel.at[side, theirs], m_send.at[side], m_recv.at[side], inner)
        for side in range(2)
    ]
    for copy in margins:
        copy.start()
    select(range(n_inner, n_inner + reach))
    for copy in margins:
        copy.wait_recv()

    base = slab * rows - MARGIN

    def key_block(q, side, slot):
        return wsel[side, jnp.clip(bands[0, slot, side, q] - base, 0, rows + 2 * MARGIN - 1)]

    lists = [(side, slot) for side in range(2) for slot in range(BAND)]

    def attend(q):
        qa_here = qa[q]
        exps, grads = [], []
        total, weighted = None, None
        for side, slot in lists:
            both = dot(key_block(q, side, slot), qa_here, NT)
            expo = jnp.where(slot < widths[side, cam], jnp.exp(both[:, :width]), 0.0)
            grad = both[:, width:]
            exps.append(expo)
            grads.append(grad)
            here = jnp.sum(expo, axis=0, keepdims=True)
            here_w = jnp.sum(expo * grad, axis=0, keepdims=True)
            total = here if total is None else total + here
            weighted = here_w if weighted is None else weighted + here_w
        inverse = 1.0 / total
        delta = weighted * inverse
        for place in range(2 * BAND):
            prob = exps[place] * inverse
            score = prob * (grads[place] - delta)
            pd[q, place] = jnp.concatenate([score.astype(BF16), prob.astype(BF16)], axis=1)

    att_copies = [pltpu.make_async_copy(att.at[q], att_out.at[0, q], out_sem.at[q]) for q in range(rows)]

    def combine(q):
        keys = jnp.concatenate([key_block(q, side, slot) for side, slot in lists], axis=0)
        pairs = pd[q, pl.ds(0, 2 * BAND)].reshape(2 * BAND * BLOCK, 2 * width)
        mixed = dot(keys, pairs, TN).astype(BF16)
        att[q] = dot(mixed[:, width:], wv[...], TN).astype(BF16)
        att_copies[q].start()
        grad_q = (dot(mixed[:, :width], wk[...], TN) * scale).astype(BF16)
        own[q] = dot(grad_q, wq[...], NT)

    for q in range(rows):
        attend(q)

    def place_of(q, side, row):
        place = jnp.int32(2 * BAND)
        for slot in range(BAND):
            place = jnp.where(bands[0, slot, side, q] - base == row, side * BAND + slot, place)
        return place

    def key_grads(first, count):
        summed = None
        for q in range(rows):
            lhs = jnp.concatenate(
                [pd[q, place_of(q, side, first + i)] for i in range(count) for side in range(2)], axis=0
            )
            part = dot(lhs, qa[q])
            summed = part if summed is None else summed + part
        return summed.reshape(count, 2, BLOCK, channels)

    back = [
        [remote(gmar.at[0], rmar.at[0], b_send.at[0], b_recv.at[0], inner)],
        [remote(gmar.at[1, i], rmar.at[1, i], b_send.at[1 + i], b_recv.at[1 + i], outer) for i in range(MARGIN)],
    ]
    for i in range(MARGIN):
        gmar[1, i] = key_grads(by_core(0, MARGIN + rows) + i, 1)[0].astype(BF16)
        back[1][i].start()
    gmar[0] = key_grads(by_core(MARGIN + rows, 0), MARGIN).astype(BF16)
    back[0][0].start()

    def totals(half, i):
        k = half * MARGIN + i
        return (
            remote(ztot.at[0, k], zin.at[0, k], y_send.at[0, k], y_recv.at[0, k], left),
            remote(ztot.at[1, k], zin.at[1, k], y_send.at[1, k], y_recv.at[1, k], right),
        )

    def relays(half, i):
        k = half * MARGIN + i
        return (
            remote(zin.at[0, k], zin.at[2, k], y_send.at[2, k], y_recv.at[2, k], left),
            remote(zin.at[1, k], zin.at[3, k], y_send.at[3, k], y_recv.at[3, k], right),
        )

    firsts = (by_core(MARGIN, 0), by_core(0, MARGIN))

    def send_row(half, i, summed):
        k = half * MARGIN + i
        ztot[:, k] = (summed[i] + rmar[half, i].astype(F32)).astype(BF16)
        for copy in totals(half, i):
            copy.start()

    def relay_half(half):
        for i in range(MARGIN):
            for copy, onward in zip(totals(half, i), relays(half, i)):
                copy.wait_recv()
                onward.start()

    first_half = key_grads(MARGIN + firsts[0], MARGIN)
    back[0][0].wait_recv()
    for i in range(MARGIN):
        send_row(0, i, first_half)
    last_half = key_grads(MARGIN + firsts[1], MARGIN)
    for q in range(rows // 2):
        combine(q)
    back[1][0].wait_recv()
    send_row(1, 0, last_half)
    combine(rows // 2)
    back[1][1].wait_recv()
    send_row(1, 1, last_half)
    relay_half(0)
    for q in range(rows // 2 + 1, rows):
        combine(q)
    relay_half(1)

    def gap_is(other, side, distance):
        other = lax.rem(other + 2 * views, views)
        gap = other - partners[0, other] if side == 0 else partners[1, other] - other
        return jnp.where(lax.rem(gap + views, views) == distance, 1, 0)

    use = (
        gap_is(cam + step, 0, step),
        gap_is(cam - step, 1, step),
        gap_is(cam + 2 * step, 0, 2 * step),
        gap_is(cam - 2 * step, 1, 2 * step),
    )
    grad_copies = [
        pltpu.make_async_copy(
            gout.at[half, i], grad_out.at[0, firsts[half] + i], out_sem.at[rows + half * MARGIN + i]
        )
        for half in range(2)
        for i in range(MARGIN)
    ]
    for half in range(2):
        for i in range(MARGIN):
            for copy in relays(half, i):
                copy.wait_recv()
            summed = own[firsts[half] + i]
            for source in range(4):
                summed = summed + jnp.where(use[source] > 0, zin[source, half * MARGIN + i].astype(F32), 0.0)
            gout[half, i] = summed.astype(BF16)
            grad_copies[half * MARGIN + i].start()

    for copy in halo_outer:
        copy.wait_send()
    halo_inner.wait_send()
    for k in range(n_inner + reach):
        for copy in (*near(k), *far(k)):
            copy.wait_send()
    for copy in (*margins, *back[0], *back[1]):
        copy.wait_send()
    for half in range(2):
        for i in range(MARGIN):
            for copy in (*totals(half, i), *relays(half, i)):
                copy.wait_send()
    for copy in (*att_copies, *grad_copies):
        copy.wait()


def local(
    views,
    slabs,
    features_in,
    conv_weight,
    q_weight,
    k_weight,
    v_weight,
    partners,
    band_widths,
    bands,
    grad_attended,
):
    _, rows, width, channels = features_in.shape
    block = (width, channels)
    chunks = rows + MARGIN
    hbm = pl.BlockSpec(memory_space=pl.ANY)
    dma = pltpu.SemaphoreType.DMA
    out = jax.ShapeDtypeStruct(features_in.shape, BF16)
    return pl.pallas_call(
        functools.partial(kernel, views, slabs),
        out_shape=(out, out),
        in_specs=[hbm] * 9,
        out_specs=(hbm, hbm),
        scratch_shapes=[
            pltpu.SMEM(partners.shape[::-1], jnp.int32),
            pltpu.SMEM(band_widths.shape[::-1], jnp.int32),
            pltpu.SMEM((1, *bands.shape[:0:-1]), jnp.int32),
            pltpu.VMEM((rows + 2 * MARGIN + 2, *block), BF16),
            pltpu.VMEM(conv_weight.shape, BF16),
            pltpu.VMEM(q_weight.shape, BF16),
            pltpu.VMEM(q_weight.shape, BF16),
            pltpu.VMEM(q_weight.shape, BF16),
            pltpu.VMEM((rows, *block), BF16),
            pltpu.VMEM((rows + 2 * MARGIN, *block), BF16),
            pltpu.VMEM((4, rows + 2 * MARGIN, *block), BF16),
            pltpu.VMEM((2, rows + 2 * MARGIN, *block), BF16),
            pltpu.VMEM((rows, 2 * width, channels), BF16),
            pltpu.VMEM((rows, 2 * BAND + 1, BLOCK, 2 * width), BF16),
            pltpu.VMEM((rows, *block), F32),
            pltpu.VMEM((2, 2, MARGIN, *block), BF16),
            pltpu.VMEM((2, 2, MARGIN, *block), BF16),
            pltpu.VMEM((2, rows, *block), BF16),
            pltpu.VMEM((4, rows, *block), BF16),
            pltpu.VMEM((rows, *block), BF16),
            pltpu.VMEM((2, MARGIN, *block), BF16),
            dma((9,)),
            dma((3,)),
            dma((3,)),
            dma((4, chunks)),
            dma((4, chunks)),
            dma((2,)),
            dma((2,)),
            dma((1 + MARGIN,)),
            dma((1 + MARGIN,)),
            dma((4, rows)),
            dma((4, rows)),
            dma((2 * rows,)),
        ],
        compiler_params=pltpu.CompilerParams(collective_id=0, has_side_effects=True),
        name="views",
    )(
        features_in,
        conv_weight,
        q_weight,
        k_weight,
        v_weight,
        partners.T,
        band_widths.T,
        bands.transpose(0, 3, 2, 1),
        grad_attended,
    )


def solution(mesh):
    placed = (
        P("cam", "row", None, None),
        P(),
        P(),
        P(),
        P(),
        P(),
        P(),
        P("cam", "row", None, None),
        P("cam", "row", None, None),
    )
    return jax.shard_map(
        functools.partial(local, mesh.shape["cam"], mesh.shape["row"]),
        mesh=mesh,
        in_specs=placed,
        out_specs=(P("cam", "row", None, None), P("cam", "row", None, None)),
        check_vma=False,
    )
```

```python
import functools

import jax
import jax.numpy as jnp
from jax import lax
from jax.experimental import pallas as pl
from jax.experimental.pallas import tpu as pltpu
from jax.sharding import PartitionSpec as P

MESH = pl.DeviceIdType.MESH
BLOCK = 128
MARGIN = 2
BAND = 3
F32 = jnp.float32
BF16 = jnp.bfloat16

NN = (((1,), (0,)), ((), ()))
NT = (((1,), (1,)), ((), ()))
TN = (((0,), (0,)), ((), ()))


def dot(a, b, dims=NN):
    return lax.dot_general(a, b, dims, preferred_element_type=F32)


def kernel(
    views,
    slabs,
    feat,
    conv_w,
    q_w,
    k_w,
    v_w,
    partners_in,
    widths_in,
    bands_in,
    grad_att,
    both_out,
    partners,
    widths,
    bands,
    fbuf,
    wconv,
    wq,
    wk,
    wv,
    dabuf,
    hwin,
    cand,
    wsel,
    qa,
    pd,
    own,
    gmar,
    rmar,
    ztot,
    zin,
    load_sem,
    halo_send,
    halo_recv,
    z_send,
    z_recv,
    m_send,
    m_recv,
    b_send,
    b_recv,
    y_send,
    y_recv,
):
    step = views // min(16, views)
    rows = dabuf.shape[0]
    width, channels = dabuf.shape[1], dabuf.shape[2]
    reach = MARGIN + 1
    cam = lax.axis_index("cam")
    slab = lax.axis_index("row")
    cam_r, cam_l = lax.rem(cam + step, views), lax.rem(cam + views - step, views)
    odd = lax.rem(slab, 2)

    def by_core(even_value, odd_value):
        return even_value + (odd_value - even_value) * odd

    inner_slab = by_core(slab + 1, slab - 1)
    outer_slab = by_core(lax.rem(slab + slabs - 1, slabs), lax.rem(slab + 1, slabs))
    right, left = (cam_r, slab), (cam_l, slab)
    inner, outer = (cam, inner_slab), (cam, outer_slab)

    barrier = pltpu.get_barrier_semaphore()
    for peer in (outer, inner, right, left):
        pl.semaphore_signal(barrier, inc=1, device_id=peer, device_id_type=MESH)

    loads = [
        pltpu.make_async_copy(feat.at[0], fbuf.at[pl.ds(reach, rows)], load_sem.at[0]),
        pltpu.make_async_copy(conv_w, wconv, load_sem.at[1]),
        pltpu.make_async_copy(grad_att.at[0], dabuf, load_sem.at[2]),
        pltpu.make_async_copy(v_w, wv, load_sem.at[3]),
        pltpu.make_async_copy(q_w, wq, load_sem.at[4]),
        pltpu.make_async_copy(k_w, wk, load_sem.at[5]),
        pltpu.make_async_copy(partners_in, partners, load_sem.at[6]),
        pltpu.make_async_copy(widths_in, widths, load_sem.at[7]),
        pltpu.make_async_copy(bands_in, bands, load_sem.at[8]),
    ]
    for load in loads:
        load.start()

    def remote(src, dst, send, recv, peer):
        return pltpu.make_async_remote_copy(
            src_ref=src, dst_ref=dst, send_sem=send, recv_sem=recv, device_id=peer, device_id_type=MESH
        )

    halo_outer = [
        remote(
            feat.at[0, by_core(0, rows - 1)],
            fbuf.at[by_core(rows + reach, reach - 1)],
            halo_send.at[0],
            halo_recv.at[0],
            outer,
        ),
        remote(
            feat.at[0, pl.ds(by_core(1, rows - reach), MARGIN)],
            fbuf.at[pl.ds(by_core(rows + reach + 1, 0), MARGIN)],
            halo_send.at[2],
            halo_recv.at[2],
            outer,
        ),
    ]
    halo_inner = remote(
        feat.at[0, by_core(rows - 1, 0)],
        fbuf.at[by_core(reach - 1, rows + reach)],
        halo_send.at[1],
        halo_recv.at[1],
        inner,
    )
    edge_row = by_core(MARGIN + rows - 1, MARGIN)
    outer_row = by_core(MARGIN, MARGIN + rows - 1)
    far_rows = by_core(0, MARGIN + rows)
    places = [*range(MARGIN + 1, MARGIN + rows - 1), edge_row, outer_row, *[far_rows + k for k in range(MARGIN)]]
    n_inner = rows - 1

    def near(k):
        r = places[k]
        return (
            remote(hwin.at[r], cand.at[0, r], z_send, z_recv.at[0, k], right),
            remote(hwin.at[r], cand.at[2, r], z_send, z_recv.at[2, k], left),
        )

    def far(k):
        r = places[k]
        return (
            remote(cand.at[0, r], cand.at[1, r], z_send, z_recv.at[1, k], right),
            remote(cand.at[2, r], cand.at[3, r], z_send, z_recv.at[3, k], left),
        )

    def conv(start, count):
        total = None
        for dy in range(3):
            weight = jnp.concatenate([wconv[dy, 0], wconv[dy, 1], wconv[dy, 2]], axis=1)
            tap = fbuf[pl.ds(start + dy, count)].reshape(count * width, channels)
            part = dot(tap, weight)
            total = part if total is None else total + part
        size = count * width
        pixel = lax.rem(lax.broadcasted_iota(jnp.int32, (size, channels), 0), width)
        before = pltpu.roll(total[:, :channels], 1, 0)
        after = pltpu.roll(total[:, 2 * channels :], size - 1, 0)
        out = total[:, channels : 2 * channels]
        out = out + jnp.where(pixel == 0, 0.0, before) + jnp.where(pixel == width - 1, 0.0, after)
        hwin[pl.ds(start, count)] = out.astype(BF16).reshape(count, width, channels)

    def relay(ks):
        for k in ks:
            for near_copy, far_copy in zip(near(k), far(k)):
                near_copy.wait_recv()
                far_copy.start()

    def launch(ks):
        for k in ks:
            for copy in near(k):
                copy.start()

    loads[0].wait()
    loads[1].wait()
    conv(MARGIN + 1, rows - 2)
    pl.semaphore_wait(barrier, 4)
    halo_outer[0].start()
    halo_inner.start()
    halo_outer[1].start()
    launch(range(rows - 2))

    loads[2].wait()
    loads[3].wait()
    loads[4].wait()
    loads[5].wait()
    grad_v = dot(dabuf[...].reshape(rows * width, channels), wv[...], NT).astype(BF16)
    qa[:, pl.ds(width, width), :] = grad_v.reshape(rows, width, channels)
    pd[:, 2 * BAND] = jnp.zeros((rows, BLOCK, 2 * width), BF16)

    halo_inner.wait_recv()
    conv(edge_row, 1)
    launch([rows - 2])
    relay([0])
    halo_outer[0].wait_recv()

    @pl.when(jnp.logical_or(slab == 0, slab == slabs - 1))
    def _():
        fbuf[by_core(reach - 1, rows + reach)] = jnp.zeros((width, channels), BF16)

    conv(outer_row, 1)
    launch([n_inner])
    halo_outer[1].wait_recv()
    conv(far_rows, MARGIN)
    launch(range(n_inner + 1, n_inner + reach))
    relay(range(1, n_inner))

    scale = channels**-0.5
    queries = dot(hwin[pl.ds(MARGIN, rows)].reshape(rows * width, channels), wq[...]).astype(BF16)
    queries = (dot(queries, wk[...], NT) * scale).astype(BF16)
    qa[:, pl.ds(0, width), :] = queries.reshape(rows, width, channels)

    for load in loads[6:]:
        load.wait()
    gap0 = lax.rem(cam - partners[0, cam] + views, views)
    gap1 = lax.rem(partners[1, cam] - cam + views, views)

    def select(ks):
        for k in ks:
            r = places[k]
            for copy in far(k):
                copy.wait_recv()
            wsel[0, r] = jnp.where(gap0 == step, cand[0, r], cand[1, r])
            wsel[1, r] = jnp.where(gap1 == step, cand[2, r], cand[3, r])

    relay(range(n_inner, n_inner + reach))
    select(range(n_inner))
    mine = pl.ds(by_core(rows, MARGIN), MARGIN)
    theirs = pl.ds(by_core(0, MARGIN + rows), MARGIN)
    margins = [
        remote(wsel.at[side, mine], wsel.at[side, theirs], m_send.at[side], m_recv.at[side], inner)
        for side in range(2)
    ]
    for copy in margins:
        copy.start()
    select(range(n_inner, n_inner + reach))
    for copy in margins:
        copy.wait_recv()

    base = slab * rows - MARGIN

    def key_block(q, side, slot):
        return wsel[side, jnp.clip(bands[0, slot, side, q] - base, 0, rows + 2 * MARGIN - 1)]

    lists = [(side, slot) for side in range(2) for slot in range(BAND)]

    def attend(q):
        qa_here = qa[q]
        exps, grads = [], []
        total, weighted = None, None
        for side, slot in lists:
            both = dot(key_block(q, side, slot), qa_here, NT)
            expo = jnp.where(slot < widths[side, cam], jnp.exp(both[:, :width]), 0.0)
            grad = both[:, width:]
            exps.append(expo)
            grads.append(grad)
            here = jnp.sum(expo, axis=0, keepdims=True)
            here_w = jnp.sum(expo * grad, axis=0, keepdims=True)
            total = here if total is None else total + here
            weighted = here_w if weighted is None else weighted + here_w
        inverse = 1.0 / total
        delta = weighted * inverse
        for place in range(2 * BAND):
            prob = exps[place] * inverse
            score = prob * (grads[place] - delta)
            pd[q, place] = jnp.concatenate([score.astype(BF16), prob.astype(BF16)], axis=1)

    def combine(q):
        keys = jnp.concatenate([key_block(q, side, slot) for side, slot in lists], axis=0)
        pairs = pd[q, pl.ds(0, 2 * BAND)].reshape(2 * BAND * BLOCK, 2 * width)
        mixed = dot(keys, pairs, TN).astype(BF16)
        both_out[0, q] = dot(mixed[:, width:], wv[...], TN).astype(BF16)
        grad_q = (dot(mixed[:, :width], wk[...], TN) * scale).astype(BF16)
        own[q] = dot(grad_q, wq[...], NT)

    for q in range(rows):
        attend(q)

    def place_of(q, side, row):
        place = jnp.int32(2 * BAND)
        for slot in range(BAND):
            place = jnp.where(bands[0, slot, side, q] - base == row, side * BAND + slot, place)
        return place

    def key_grads(first, count):
        summed = None
        for q in range(rows):
            lhs = jnp.concatenate(
                [pd[q, place_of(q, side, first + i)] for i in range(count) for side in range(2)], axis=0
            )
            part = dot(lhs, qa[q])
            summed = part if summed is None else summed + part
        return summed.reshape(count, 2, BLOCK, channels)

    back = [
        [remote(gmar.at[0], rmar.at[0], b_send.at[0], b_recv.at[0], inner)],
        [remote(gmar.at[1, i], rmar.at[1, i], b_send.at[1 + i], b_recv.at[1 + i], outer) for i in range(MARGIN)],
    ]
    for i in range(MARGIN):
        gmar[1, i] = key_grads(by_core(0, MARGIN + rows) + i, 1)[0].astype(BF16)
        back[1][i].start()
    gmar[0] = key_grads(by_core(MARGIN + rows, 0), MARGIN).astype(BF16)
    back[0][0].start()

    def totals(half, i):
        k = half * MARGIN + i
        return (
            remote(ztot.at[0, k], zin.at[0, k], y_send, y_recv.at[0, k], left),
            remote(ztot.at[1, k], zin.at[1, k], y_send, y_recv.at[1, k], right),
        )

    def relays(half, i):
        k = half * MARGIN + i
        return (
            remote(zin.at[0, k], zin.at[2, k], y_send, y_recv.at[2, k], left),
            remote(zin.at[1, k], zin.at[3, k], y_send, y_recv.at[3, k], right),
        )

    firsts = (by_core(MARGIN, 0), by_core(0, MARGIN))

    def send_row(half, i, summed):
        k = half * MARGIN + i
        ztot[:, k] = (summed[i] + rmar[half, i].astype(F32)).astype(BF16)
        for copy in totals(half, i):
            copy.start()

    def relay_half(half):
        for i in range(MARGIN):
            for copy, onward in zip(totals(half, i), relays(half, i)):
                copy.wait_recv()
                onward.start()

    first_half = key_grads(MARGIN + firsts[0], MARGIN)
    back[0][0].wait_recv()
    for i in range(MARGIN):
        send_row(0, i, first_half)
    last_half = key_grads(MARGIN + firsts[1], MARGIN)
    for q in range(rows // 2):
        combine(q)
    back[1][0].wait_recv()
    send_row(1, 0, last_half)
    combine(rows // 2)
    back[1][1].wait_recv()
    send_row(1, 1, last_half)
    relay_half(0)
    for q in range(rows // 2 + 1, rows):
        combine(q)
    relay_half(1)

    def gap_is(other, side, distance):
        other = lax.rem(other + 2 * views, views)
        gap = other - partners[0, other] if side == 0 else partners[1, other] - other
        return jnp.where(lax.rem(gap + views, views) == distance, 1, 0)

    use = (
        gap_is(cam + step, 0, step),
        gap_is(cam - step, 1, step),
        gap_is(cam + 2 * step, 0, 2 * step),
        gap_is(cam - 2 * step, 1, 2 * step),
    )
    for half in range(2):
        for i in range(MARGIN):
            for copy in relays(half, i):
                copy.wait_recv()
            summed = own[firsts[half] + i]
            for source in range(4):
                summed = summed + jnp.where(use[source] > 0, zin[source, half * MARGIN + i].astype(F32), 0.0)
            both_out[1, firsts[half] + i] = summed.astype(BF16)

    for copy in halo_outer:
        copy.wait_send()
    halo_inner.wait_send()
    sent = cand.at[:, pl.ds(0, n_inner + reach)]
    pltpu.make_async_copy(sent, sent, z_send).wait()
    for copy in (*margins, *back[0], *back[1]):
        copy.wait_send()
    pltpu.make_async_copy(zin, zin, y_send).wait()


def local(
    views,
    slabs,
    features_in,
    conv_weight,
    q_weight,
    k_weight,
    v_weight,
    partners,
    band_widths,
    bands,
    grad_attended,
):
    _, rows, width, channels = features_in.shape
    block = (width, channels)
    chunks = rows + MARGIN
    hbm = pl.BlockSpec(memory_space=pl.ANY)
    dma = pltpu.SemaphoreType.DMA
    out = jax.ShapeDtypeStruct((2, *features_in.shape[1:]), BF16)
    both = pl.pallas_call(
        functools.partial(kernel, views, slabs),
        out_shape=out,
        in_specs=[hbm] * 9,
        out_specs=pl.BlockSpec(memory_space=pltpu.VMEM),
        scratch_shapes=[
            pltpu.SMEM(partners.shape[::-1], jnp.int32),
            pltpu.SMEM(band_widths.shape[::-1], jnp.int32),
            pltpu.SMEM((1, *bands.shape[:0:-1]), jnp.int32),
            pltpu.VMEM((rows + 2 * MARGIN + 2, *block), BF16),
            pltpu.VMEM(conv_weight.shape, BF16),
            pltpu.VMEM(q_weight.shape, BF16),
            pltpu.VMEM(q_weight.shape, BF16),
            pltpu.VMEM(q_weight.shape, BF16),
            pltpu.VMEM((rows, *block), BF16),
            pltpu.VMEM((rows + 2 * MARGIN, *block), BF16),
            pltpu.VMEM((4, rows + 2 * MARGIN, *block), BF16),
            pltpu.VMEM((2, rows + 2 * MARGIN, *block), BF16),
            pltpu.VMEM((rows, 2 * width, channels), BF16),
            pltpu.VMEM((rows, 2 * BAND + 1, BLOCK, 2 * width), BF16),
            pltpu.VMEM((rows, *block), F32),
            pltpu.VMEM((2, 2, MARGIN, *block), BF16),
            pltpu.VMEM((2, 2, MARGIN, *block), BF16),
            pltpu.VMEM((2, rows, *block), BF16),
            pltpu.VMEM((4, rows, *block), BF16),
            dma((9,)),
            dma((3,)),
            dma((3,)),
            dma,
            dma((4, chunks)),
            dma((2,)),
            dma((2,)),
            dma((1 + MARGIN,)),
            dma((1 + MARGIN,)),
            dma,
            dma((4, rows)),
        ],
        compiler_params=pltpu.CompilerParams(collective_id=0, has_side_effects=True, vmem_limit_bytes=32 << 20),
        name="views",
    )(
        *[
            pltpu.with_memory_space_constraint(array, pltpu.HBM)
            for array in (
                features_in,
                conv_weight,
                q_weight,
                k_weight,
                v_weight,
                partners.T,
                band_widths.T,
                bands.transpose(0, 3, 2, 1),
                grad_attended,
            )
        ]
    )
    return both[:1], both[1:]


def solution(mesh):
    placed = (
        P("cam", "row", None, None),
        P(),
        P(),
        P(),
        P(),
        P(),
        P(),
        P("cam", "row", None, None),
        P("cam", "row", None, None),
    )
    return jax.shard_map(
        functools.partial(local, mesh.shape["cam"], mesh.shape["row"]),
        mesh=mesh,
        in_specs=placed,
        out_specs=(P("cam", "row", None, None), P("cam", "row", None, None)),
        check_vma=False,
    )
```

```python
import functools

import jax
import jax.numpy as jnp
from jax import lax
from jax.experimental import pallas as pl
from jax.experimental.pallas import tpu as pltpu
from jax.sharding import PartitionSpec as P

MESH = pl.DeviceIdType.MESH
BLOCK = 128
MARGIN = 2
BAND = 3
F32 = jnp.float32
BF16 = jnp.bfloat16

NN = (((1,), (0,)), ((), ()))
NT = (((1,), (1,)), ((), ()))
TN = (((0,), (0,)), ((), ()))


def dot(a, b, dims=NN):
    return lax.dot_general(a, b, dims, preferred_element_type=F32)


def kernel(
    views,
    slabs,
    feat,
    conv_w,
    q_w,
    k_w,
    v_w,
    partners_in,
    widths_in,
    bands_in,
    grad_att,
    both_out,
    partners,
    widths,
    bands,
    fbuf,
    wconv,
    wq,
    wk,
    wv,
    dabuf,
    hwin,
    cand,
    wsel,
    qa,
    pd,
    own,
    gmar,
    rmar,
    ztot,
    zin,
    load_sem,
    halo_send,
    halo_recv,
    z_send,
    z_recv,
    m_send,
    m_recv,
    b_send,
    b_recv,
    y_send,
    y_recv,
):
    step = views // min(16, views)
    rows = dabuf.shape[0]
    width, channels = dabuf.shape[1], dabuf.shape[2]
    reach = MARGIN + 1
    cam = lax.axis_index("cam")
    slab = lax.axis_index("row")
    cam_r, cam_l = lax.rem(cam + step, views), lax.rem(cam + views - step, views)
    odd = lax.rem(slab, 2)

    def by_core(even_value, odd_value):
        return even_value + (odd_value - even_value) * odd

    inner_slab = by_core(slab + 1, slab - 1)
    outer_slab = by_core(lax.rem(slab + slabs - 1, slabs), lax.rem(slab + 1, slabs))
    right, left = (cam_r, slab), (cam_l, slab)
    inner, outer = (cam, inner_slab), (cam, outer_slab)

    barrier = pltpu.get_barrier_semaphore()
    for peer in (outer, inner, right, left):
        pl.semaphore_signal(barrier, inc=1, device_id=peer, device_id_type=MESH)

    loads = [
        pltpu.make_async_copy(feat.at[0], fbuf.at[pl.ds(reach, rows)], load_sem.at[0]),
        pltpu.make_async_copy(conv_w, wconv, load_sem.at[1]),
        pltpu.make_async_copy(grad_att.at[0], dabuf, load_sem.at[2]),
        pltpu.make_async_copy(v_w, wv, load_sem.at[3]),
        pltpu.make_async_copy(q_w, wq, load_sem.at[4]),
        pltpu.make_async_copy(k_w, wk, load_sem.at[5]),
        pltpu.make_async_copy(partners_in, partners, load_sem.at[6]),
        pltpu.make_async_copy(widths_in, widths, load_sem.at[7]),
        pltpu.make_async_copy(bands_in, bands, load_sem.at[8]),
    ]
    for load in loads:
        load.start()

    def remote(src, dst, send, recv, peer):
        return pltpu.make_async_remote_copy(
            src_ref=src, dst_ref=dst, send_sem=send, recv_sem=recv, device_id=peer, device_id_type=MESH
        )

    halo_outer = [
        remote(
            feat.at[0, by_core(0, rows - 1)],
            fbuf.at[by_core(rows + reach, reach - 1)],
            halo_send.at[0],
            halo_recv.at[0],
            outer,
        ),
        remote(
            feat.at[0, by_core(1, rows - MARGIN)],
            fbuf.at[by_core(rows + reach + 1, reach - MARGIN)],
            halo_send.at[2],
            halo_recv.at[2],
            outer,
        ),
    ]
    halo_inner = remote(
        feat.at[0, by_core(rows - 1, 0)],
        fbuf.at[by_core(reach - 1, rows + reach)],
        halo_send.at[1],
        halo_recv.at[1],
        inner,
    )
    edge_row = by_core(MARGIN + rows - 1, MARGIN)
    outer_row = by_core(MARGIN, MARGIN + rows - 1)
    margin_row = by_core(MARGIN - 1, MARGIN + rows)
    places = [by_core(MARGIN + 1, MARGIN + 2), by_core(MARGIN + 2, MARGIN + 1), edge_row, outer_row, margin_row]
    n_inner = rows - 1

    def near(k):
        r = places[k]
        return (
            remote(hwin.at[r], cand.at[0, r], z_send, z_recv.at[0, k], right),
            remote(hwin.at[r], cand.at[2, r], z_send, z_recv.at[2, k], left),
        )

    def far(k):
        r = places[k]
        return (
            remote(cand.at[0, r], cand.at[1, r], z_send, z_recv.at[1, k], right),
            remote(cand.at[2, r], cand.at[3, r], z_send, z_recv.at[3, k], left),
        )

    def conv(start, count):
        total = None
        for dy in range(3):
            weight = jnp.concatenate([wconv[dy, 0], wconv[dy, 1], wconv[dy, 2]], axis=1)
            tap = fbuf[pl.ds(start + dy, count)].reshape(count * width, channels)
            part = dot(tap, weight)
            total = part if total is None else total + part
        size = count * width
        pixel = lax.rem(lax.broadcasted_iota(jnp.int32, (size, channels), 0), width)
        before = pltpu.roll(total[:, :channels], 1, 0)
        after = pltpu.roll(total[:, 2 * channels :], size - 1, 0)
        out = total[:, channels : 2 * channels]
        out = out + jnp.where(pixel == 0, 0.0, before) + jnp.where(pixel == width - 1, 0.0, after)
        hwin[pl.ds(start, count)] = out.astype(BF16).reshape(count, width, channels)

    def relay(ks):
        for k in ks:
            for near_copy, far_copy in zip(near(k), far(k)):
                near_copy.wait_recv()
                far_copy.start()

    def launch(ks):
        for k in ks:
            for copy in near(k):
                copy.start()

    loads[0].wait()
    loads[1].wait()
    conv(MARGIN + 1, rows - 2)
    pl.semaphore_wait(barrier, 4)
    halo_outer[0].start()
    halo_inner.start()
    halo_outer[1].start()
    launch(range(rows - 2))

    loads[2].wait()
    loads[3].wait()
    loads[4].wait()
    loads[5].wait()
    grad_v = dot(dabuf[...].reshape(rows * width, channels), wv[...], NT).astype(BF16)
    qa[:, pl.ds(width, width), :] = grad_v.reshape(rows, width, channels)
    pd[:, 2 * BAND] = jnp.zeros((rows, BLOCK, 2 * width), BF16)

    halo_inner.wait_recv()
    conv(edge_row, 1)
    launch([rows - 2])
    relay([0])
    halo_outer[0].wait_recv()

    @pl.when(jnp.logical_or(slab == 0, slab == slabs - 1))
    def _():
        fbuf[by_core(reach - 1, rows + reach)] = jnp.zeros((width, channels), BF16)

    conv(outer_row, 1)
    launch([n_inner])
    halo_outer[1].wait_recv()
    conv(margin_row, 1)
    launch([n_inner + 1])
    relay(range(1, n_inner))

    scale = channels**-0.5
    queries = dot(hwin[pl.ds(MARGIN, rows)].reshape(rows * width, channels), wq[...]).astype(BF16)
    queries = (dot(queries, wk[...], NT) * scale).astype(BF16)
    qa[:, pl.ds(0, width), :] = queries.reshape(rows, width, channels)

    for load in loads[6:]:
        load.wait()
    gap0 = lax.rem(cam - partners[0, cam] + views, views)
    gap1 = lax.rem(partners[1, cam] - cam + views, views)

    def select(ks):
        for k in ks:
            r = places[k]
            for copy in far(k):
                copy.wait_recv()
            wsel[0, r] = jnp.where(gap0 == step, cand[0, r], cand[1, r])
            wsel[1, r] = jnp.where(gap1 == step, cand[2, r], cand[3, r])

    select([0])
    crossing = [
        remote(
            wsel.at[side, places[0]],
            wsel.at[side, by_core(2 * MARGIN + rows - 1, 0)],
            m_send.at[2 + side],
            m_recv.at[2 + side],
            outer,
        )
        for side in range(2)
    ]
    for copy in crossing:
        copy.start()
    relay(range(n_inner, n_inner + 2))
    select(range(1, n_inner))
    mine = pl.ds(by_core(rows, MARGIN), MARGIN)
    theirs = pl.ds(by_core(0, MARGIN + rows), MARGIN)
    margins = [
        remote(wsel.at[side, mine], wsel.at[side, theirs], m_send.at[side], m_recv.at[side], inner)
        for side in range(2)
    ]
    for copy in margins:
        copy.start()
    select(range(n_inner, n_inner + 2))
    for copy in (*margins, *crossing):
        copy.wait_recv()

    base = slab * rows - MARGIN

    def key_block(q, side, slot):
        return wsel[side, jnp.clip(bands[0, slot, side, q] - base, 0, rows + 2 * MARGIN - 1)]

    lists = [(side, slot) for side in range(2) for slot in range(BAND)]

    def attend(q):
        qa_here = qa[q]
        exps, grads = [], []
        total, weighted = None, None
        for side, slot in lists:
            both = dot(key_block(q, side, slot), qa_here, NT)
            expo = jnp.where(slot < widths[side, cam], jnp.exp(both[:, :width]), 0.0)
            grad = both[:, width:]
            exps.append(expo)
            grads.append(grad)
            here = jnp.sum(expo, axis=0, keepdims=True)
            here_w = jnp.sum(expo * grad, axis=0, keepdims=True)
            total = here if total is None else total + here
            weighted = here_w if weighted is None else weighted + here_w
        inverse = 1.0 / total
        delta = weighted * inverse
        for place in range(2 * BAND):
            prob = exps[place] * inverse
            score = prob * (grads[place] - delta)
            pd[q, place] = jnp.concatenate([score.astype(BF16), prob.astype(BF16)], axis=1)

    def combine(q):
        keys = jnp.concatenate([key_block(q, side, slot) for side, slot in lists], axis=0)
        pairs = pd[q, pl.ds(0, 2 * BAND)].reshape(2 * BAND * BLOCK, 2 * width)
        mixed = dot(keys, pairs, TN).astype(BF16)
        both_out[0, q] = dot(mixed[:, width:], wv[...], TN).astype(BF16)
        grad_q = (dot(mixed[:, :width], wk[...], TN) * scale).astype(BF16)
        own[q] = dot(grad_q, wq[...], NT)

    for q in range(rows):
        attend(q)

    def place_of(q, side, row):
        place = jnp.int32(2 * BAND)
        for slot in range(BAND):
            place = jnp.where(bands[0, slot, side, q] - base == row, side * BAND + slot, place)
        return place

    def key_grads(first, count):
        summed = None
        for q in range(rows):
            lhs = jnp.concatenate(
                [pd[q, place_of(q, side, first + i)] for i in range(count) for side in range(2)], axis=0
            )
            part = dot(lhs, qa[q])
            summed = part if summed is None else summed + part
        return summed.reshape(count, 2, BLOCK, channels)

    back = [
        [remote(gmar.at[0], rmar.at[0], b_send.at[0], b_recv.at[0], inner)],
        [remote(gmar.at[1, i], rmar.at[1, i], b_send.at[1 + i], b_recv.at[1 + i], outer) for i in range(MARGIN)],
    ]
    for i in range(MARGIN):
        gmar[1, i] = key_grads(by_core(0, MARGIN + rows) + i, 1)[0].astype(BF16)
        back[1][i].start()
    gmar[0] = key_grads(by_core(MARGIN + rows, 0), MARGIN).astype(BF16)
    back[0][0].start()

    def totals(half, i):
        k = half * MARGIN + i
        return (
            remote(ztot.at[0, k], zin.at[0, k], y_send, y_recv.at[0, k], left),
            remote(ztot.at[1, k], zin.at[1, k], y_send, y_recv.at[1, k], right),
        )

    def relays(half, i):
        k = half * MARGIN + i
        return (
            remote(zin.at[0, k], zin.at[2, k], y_send, y_recv.at[2, k], left),
            remote(zin.at[1, k], zin.at[3, k], y_send, y_recv.at[3, k], right),
        )

    firsts = (by_core(MARGIN, 0), by_core(0, MARGIN))

    def send_row(half, i, summed):
        k = half * MARGIN + i
        ztot[:, k] = (summed[i] + rmar[half, i].astype(F32)).astype(BF16)
        for copy in totals(half, i):
            copy.start()

    def relay_half(half):
        for i in range(MARGIN):
            for copy, onward in zip(totals(half, i), relays(half, i)):
                copy.wait_recv()
                onward.start()

    first_half = key_grads(MARGIN + firsts[0], MARGIN)
    back[0][0].wait_recv()
    for i in range(MARGIN):
        send_row(0, i, first_half)
    last_half = key_grads(MARGIN + firsts[1], MARGIN)
    for q in range(rows // 2):
        combine(q)
    back[1][0].wait_recv()
    send_row(1, 0, last_half)
    combine(rows // 2)
    back[1][1].wait_recv()
    send_row(1, 1, last_half)
    relay_half(0)
    for q in range(rows // 2 + 1, rows):
        combine(q)
    relay_half(1)

    def gap_is(other, side, distance):
        other = lax.rem(other + 2 * views, views)
        gap = other - partners[0, other] if side == 0 else partners[1, other] - other
        return jnp.where(lax.rem(gap + views, views) == distance, 1, 0)

    use = (
        gap_is(cam + step, 0, step),
        gap_is(cam - step, 1, step),
        gap_is(cam + 2 * step, 0, 2 * step),
        gap_is(cam - 2 * step, 1, 2 * step),
    )
    for half in range(2):
        for i in range(MARGIN):
            for copy in relays(half, i):
                copy.wait_recv()
            summed = own[firsts[half] + i]
            for source in range(4):
                summed = summed + jnp.where(use[source] > 0, zin[source, half * MARGIN + i].astype(F32), 0.0)
            both_out[1, firsts[half] + i] = summed.astype(BF16)

    for copy in halo_outer:
        copy.wait_send()
    halo_inner.wait_send()
    sent = cand.at[:, pl.ds(0, n_inner + 2)]
    pltpu.make_async_copy(sent, sent, z_send).wait()
    for copy in (*margins, *crossing, *back[0], *back[1]):
        copy.wait_send()
    pltpu.make_async_copy(zin, zin, y_send).wait()


def local(
    views,
    slabs,
    features_in,
    conv_weight,
    q_weight,
    k_weight,
    v_weight,
    partners,
    band_widths,
    bands,
    grad_attended,
):
    _, rows, width, channels = features_in.shape
    block = (width, channels)
    chunks = rows + 1
    hbm = pl.BlockSpec(memory_space=pl.ANY)
    dma = pltpu.SemaphoreType.DMA
    out = jax.ShapeDtypeStruct((2, *features_in.shape[1:]), BF16)
    both = pl.pallas_call(
        functools.partial(kernel, views, slabs),
        out_shape=out,
        in_specs=[hbm] * 9,
        out_specs=pl.BlockSpec(memory_space=pltpu.VMEM),
        scratch_shapes=[
            pltpu.SMEM(partners.shape[::-1], jnp.int32),
            pltpu.SMEM(band_widths.shape[::-1], jnp.int32),
            pltpu.SMEM((1, *bands.shape[:0:-1]), jnp.int32),
            pltpu.VMEM((rows + 2 * MARGIN + 2, *block), BF16),
            pltpu.VMEM(conv_weight.shape, BF16),
            pltpu.VMEM(q_weight.shape, BF16),
            pltpu.VMEM(q_weight.shape, BF16),
            pltpu.VMEM(q_weight.shape, BF16),
            pltpu.VMEM((rows, *block), BF16),
            pltpu.VMEM((rows + 2 * MARGIN, *block), BF16),
            pltpu.VMEM((4, rows + 2 * MARGIN, *block), BF16),
            pltpu.VMEM((2, rows + 2 * MARGIN, *block), BF16),
            pltpu.VMEM((rows, 2 * width, channels), BF16),
            pltpu.VMEM((rows, 2 * BAND + 1, BLOCK, 2 * width), BF16),
            pltpu.VMEM((rows, *block), F32),
            pltpu.VMEM((2, 2, MARGIN, *block), BF16),
            pltpu.VMEM((2, 2, MARGIN, *block), BF16),
            pltpu.VMEM((2, rows, *block), BF16),
            pltpu.VMEM((4, rows, *block), BF16),
            dma((9,)),
            dma((3,)),
            dma((3,)),
            dma,
            dma((4, chunks)),
            dma((4,)),
            dma((4,)),
            dma((1 + MARGIN,)),
            dma((1 + MARGIN,)),
            dma,
            dma((4, rows)),
        ],
        compiler_params=pltpu.CompilerParams(collective_id=0, has_side_effects=True, vmem_limit_bytes=32 << 20),
        name="views",
    )(
        *[
            pltpu.with_memory_space_constraint(array, pltpu.HBM)
            for array in (
                features_in,
                conv_weight,
                q_weight,
                k_weight,
                v_weight,
                partners.T,
                band_widths.T,
                bands.transpose(0, 3, 2, 1),
                grad_attended,
            )
        ]
    )
    return both[:1], both[1:]


def solution(mesh):
    placed = (
        P("cam", "row", None, None),
        P(),
        P(),
        P(),
        P(),
        P(),
        P(),
        P("cam", "row", None, None),
        P("cam", "row", None, None),
    )
    return jax.shard_map(
        functools.partial(local, mesh.shape["cam"], mesh.shape["row"]),
        mesh=mesh,
        in_specs=placed,
        out_specs=(P("cam", "row", None, None), P("cam", "row", None, None)),
        check_vma=False,
    )
```

```python
import functools

import jax
import jax.numpy as jnp
from jax import lax
from jax.experimental import pallas as pl
from jax.experimental.pallas import tpu as pltpu
from jax.sharding import PartitionSpec as P

MESH = pl.DeviceIdType.MESH
BLOCK = 128
MARGIN = 2
BAND = 3
F32 = jnp.float32
BF16 = jnp.bfloat16

NN = (((1,), (0,)), ((), ()))
NT = (((1,), (1,)), ((), ()))
TN = (((0,), (0,)), ((), ()))


def dot(a, b, dims=NN):
    return lax.dot_general(a, b, dims, preferred_element_type=F32)


def kernel(
    views,
    slabs,
    feat,
    conv_w,
    q_w,
    k_w,
    v_w,
    partners_in,
    widths_in,
    bands_in,
    grad_att,
    both_out,
    partners,
    widths,
    bands,
    fbuf,
    wconv,
    wq,
    wk,
    wv,
    dabuf,
    hwin,
    cand,
    wsel,
    qa,
    pd,
    own,
    gmar,
    rmar,
    ztot,
    zin,
    xout,
    xin,
    load_sem,
    halo_send,
    halo_recv,
    z_send,
    z_recv,
    m_send,
    m_recv,
    b_send,
    b_recv,
    y_send,
    y_recv,
):
    step = views // min(16, views)
    rows = dabuf.shape[0]
    width, channels = dabuf.shape[1], dabuf.shape[2]
    reach = MARGIN + 1
    cam = lax.axis_index("cam")
    slab = lax.axis_index("row")
    cam_r, cam_l = lax.rem(cam + step, views), lax.rem(cam + views - step, views)
    odd = lax.rem(slab, 2)

    def by_core(even_value, odd_value):
        return even_value + (odd_value - even_value) * odd

    inner_slab = by_core(slab + 1, slab - 1)
    outer_slab = by_core(lax.rem(slab + slabs - 1, slabs), lax.rem(slab + 1, slabs))
    right, left = (cam_r, slab), (cam_l, slab)
    inner, outer = (cam, inner_slab), (cam, outer_slab)

    barrier = pltpu.get_barrier_semaphore()
    for peer in (outer, inner, right, left):
        pl.semaphore_signal(barrier, inc=1, device_id=peer, device_id_type=MESH)

    loads = [
        pltpu.make_async_copy(feat.at[0], fbuf.at[pl.ds(reach, rows)], load_sem.at[0]),
        pltpu.make_async_copy(conv_w, wconv, load_sem.at[1]),
        pltpu.make_async_copy(grad_att.at[0], dabuf, load_sem.at[2]),
        pltpu.make_async_copy(v_w, wv, load_sem.at[3]),
        pltpu.make_async_copy(q_w, wq, load_sem.at[4]),
        pltpu.make_async_copy(k_w, wk, load_sem.at[5]),
        pltpu.make_async_copy(partners_in, partners, load_sem.at[6]),
        pltpu.make_async_copy(widths_in, widths, load_sem.at[7]),
        pltpu.make_async_copy(bands_in, bands, load_sem.at[8]),
    ]
    for load in loads:
        load.start()

    def remote(src, dst, send, recv, peer):
        return pltpu.make_async_remote_copy(
            src_ref=src, dst_ref=dst, send_sem=send, recv_sem=recv, device_id=peer, device_id_type=MESH
        )

    halo_outer = [
        remote(
            feat.at[0, by_core(0, rows - 1)],
            fbuf.at[by_core(rows + reach, reach - 1)],
            halo_send.at[0],
            halo_recv.at[0],
            outer,
        ),
        remote(
            feat.at[0, by_core(1, rows - MARGIN)],
            fbuf.at[by_core(rows + reach + 1, reach - MARGIN)],
            halo_send.at[2],
            halo_recv.at[2],
            outer,
        ),
    ]
    halo_inner = remote(
        feat.at[0, by_core(rows - 1, 0)],
        fbuf.at[by_core(reach - 1, rows + reach)],
        halo_send.at[1],
        halo_recv.at[1],
        inner,
    )
    edge_row = by_core(MARGIN + rows - 1, MARGIN)
    outer_row = by_core(MARGIN, MARGIN + rows - 1)
    margin_row = by_core(MARGIN - 1, MARGIN + rows)
    places = [by_core(MARGIN + 1, MARGIN + 2), by_core(MARGIN + 2, MARGIN + 1), edge_row, outer_row, margin_row]
    n_inner = rows - 1

    def near(k):
        r = places[k]
        return (
            remote(hwin.at[r], cand.at[0, r], z_send, z_recv.at[0, k], right),
            remote(hwin.at[r], cand.at[2, r], z_send, z_recv.at[2, k], left),
        )

    def far(k):
        r = places[k]
        return (
            remote(cand.at[0, r], cand.at[1, r], z_send, z_recv.at[1, k], right),
            remote(cand.at[2, r], cand.at[3, r], z_send, z_recv.at[3, k], left),
        )

    def conv(start, count):
        total = None
        for dy in range(3):
            weight = jnp.concatenate([wconv[dy, 0], wconv[dy, 1], wconv[dy, 2]], axis=1)
            tap = fbuf[pl.ds(start + dy, count)].reshape(count * width, channels)
            part = dot(tap, weight)
            total = part if total is None else total + part
        size = count * width
        pixel = lax.rem(lax.broadcasted_iota(jnp.int32, (size, channels), 0), width)
        before = pltpu.roll(total[:, :channels], 1, 0)
        after = pltpu.roll(total[:, 2 * channels :], size - 1, 0)
        out = total[:, channels : 2 * channels]
        out = out + jnp.where(pixel == 0, 0.0, before) + jnp.where(pixel == width - 1, 0.0, after)
        hwin[pl.ds(start, count)] = out.astype(BF16).reshape(count, width, channels)

    def relay(ks):
        for k in ks:
            for near_copy, far_copy in zip(near(k), far(k)):
                near_copy.wait_recv()
                far_copy.start()

    def launch(ks):
        for k in ks:
            for copy in near(k):
                copy.start()

    loads[0].wait()
    loads[1].wait()
    conv(MARGIN + 1, rows - 2)
    pl.semaphore_wait(barrier, 4)
    halo_outer[0].start()
    halo_inner.start()
    halo_outer[1].start()
    launch(range(rows - 2))

    loads[2].wait()
    loads[3].wait()
    loads[4].wait()
    loads[5].wait()
    grad_v = dot(dabuf[...].reshape(rows * width, channels), wv[...], NT).astype(BF16)
    qa[:, pl.ds(width, width), :] = grad_v.reshape(rows, width, channels)
    pd[:, 2 * BAND] = jnp.zeros((rows, BLOCK, 2 * width), BF16)

    halo_inner.wait_recv()
    conv(edge_row, 1)
    launch([rows - 2])
    relay([0])
    halo_outer[0].wait_recv()

    @pl.when(jnp.logical_or(slab == 0, slab == slabs - 1))
    def _():
        fbuf[by_core(reach - 1, rows + reach)] = jnp.zeros((width, channels), BF16)

    conv(outer_row, 1)
    launch([n_inner])
    halo_outer[1].wait_recv()
    conv(margin_row, 1)
    launch([n_inner + 1])
    relay(range(1, n_inner))

    scale = channels**-0.5
    queries = dot(hwin[pl.ds(MARGIN, rows)].reshape(rows * width, channels), wq[...]).astype(BF16)
    queries = (dot(queries, wk[...], NT) * scale).astype(BF16)
    qa[:, pl.ds(0, width), :] = queries.reshape(rows, width, channels)

    for load in loads[6:]:
        load.wait()
    gap0 = lax.rem(cam - partners[0, cam] + views, views)
    gap1 = lax.rem(partners[1, cam] - cam + views, views)

    def select(ks):
        for k in ks:
            r = places[k]
            for copy in far(k):
                copy.wait_recv()
            wsel[0, r] = jnp.where(gap0 == step, cand[0, r], cand[1, r])
            wsel[1, r] = jnp.where(gap1 == step, cand[2, r], cand[3, r])

    select([0])
    crossing = [
        remote(
            wsel.at[side, places[0]],
            wsel.at[side, by_core(2 * MARGIN + rows - 1, 0)],
            m_send.at[2 + side],
            m_recv.at[2 + side],
            outer,
        )
        for side in range(2)
    ]
    for copy in crossing:
        copy.start()
    relay(range(n_inner, n_inner + 2))
    select(range(1, n_inner))
    mine = pl.ds(by_core(rows, MARGIN), MARGIN)
    theirs = pl.ds(by_core(0, MARGIN + rows), MARGIN)
    margins = [
        remote(wsel.at[side, mine], wsel.at[side, theirs], m_send.at[side], m_recv.at[side], inner)
        for side in range(2)
    ]
    for copy in margins:
        copy.start()
    select(range(n_inner, n_inner + 2))
    for copy in (*margins, *crossing):
        copy.wait_recv()

    base = slab * rows - MARGIN

    def key_block(q, side, slot):
        return wsel[side, jnp.clip(bands[0, slot, side, q] - base, 0, rows + 2 * MARGIN - 1)]

    lists = [(side, slot) for side in range(2) for slot in range(BAND)]

    def attend(q):
        qa_here = qa[q]
        exps, grads = [], []
        total, weighted = None, None
        for side, slot in lists:
            both = dot(key_block(q, side, slot), qa_here, NT)
            expo = jnp.where(slot < widths[side, cam], jnp.exp(both[:, :width]), 0.0)
            grad = both[:, width:]
            exps.append(expo)
            grads.append(grad)
            here = jnp.sum(expo, axis=0, keepdims=True)
            here_w = jnp.sum(expo * grad, axis=0, keepdims=True)
            total = here if total is None else total + here
            weighted = here_w if weighted is None else weighted + here_w
        inverse = 1.0 / total
        delta = weighted * inverse
        for place in range(2 * BAND):
            prob = exps[place] * inverse
            score = prob * (grads[place] - delta)
            pd[q, place] = jnp.concatenate([score.astype(BF16), prob.astype(BF16)], axis=1)

    def combine(q):
        keys = jnp.concatenate([key_block(q, side, slot) for side, slot in lists], axis=0)
        pairs = pd[q, pl.ds(0, 2 * BAND)].reshape(2 * BAND * BLOCK, 2 * width)
        mixed = dot(keys, pairs, TN).astype(BF16)
        both_out[0, q] = dot(mixed[:, width:], wv[...], TN).astype(BF16)
        grad_q = (dot(mixed[:, :width], wk[...], TN) * scale).astype(BF16)
        own[q] = dot(grad_q, wq[...], NT)

    for q in range(rows):
        attend(q)

    def place_of(q, side, row):
        place = jnp.int32(2 * BAND)
        for slot in range(BAND):
            place = jnp.where(bands[0, slot, side, q] - base == row, side * BAND + slot, place)
        return place

    def key_grads(first, count):
        summed = None
        for q in range(rows):
            lhs = jnp.concatenate(
                [pd[q, place_of(q, side, first + i)] for i in range(count) for side in range(2)], axis=0
            )
            part = dot(lhs, qa[q])
            summed = part if summed is None else summed + part
        return summed.reshape(count, 2, BLOCK, channels)

    near_half = by_core(MARGIN, 0)
    own_rows = [None, near_half, near_half + 1, by_core(1, rows - MARGIN), by_core(0, rows - 1)]
    back_inner = remote(gmar.at[pl.ds(0, MARGIN)], rmar.at[pl.ds(0, MARGIN)], b_send.at[0], b_recv.at[0], inner)
    back_outer = remote(gmar.at[MARGIN], rmar.at[MARGIN], b_send.at[1], b_recv.at[1], outer)
    back_cross = remote(xout, xin, b_send.at[2], b_recv.at[2], outer)

    def totals(k):
        return (
            remote(ztot.at[0, k], zin.at[0, k], y_send, y_recv.at[0, k], left),
            remote(ztot.at[1, k], zin.at[1, k], y_send, y_recv.at[1, k], right),
        )

    def relays(k):
        return (
            remote(zin.at[0, k], zin.at[2, k], y_send, y_recv.at[2, k], left),
            remote(zin.at[1, k], zin.at[3, k], y_send, y_recv.at[3, k], right),
        )

    def send_row(k, summed):
        ztot[:, k] = summed.astype(BF16)
        for copy in totals(k):
            copy.start()

    def relay_row(k):
        for copy, onward in zip(totals(k), relays(k)):
            copy.wait_recv()
            onward.start()

    gmar[MARGIN] = key_grads(by_core(MARGIN - 1, MARGIN + rows), 1)[0].astype(BF16)
    back_outer.start()
    send_row(0, key_grads(by_core(0, 2 * MARGIN + rows - 1), 1)[0])
    gmar[pl.ds(0, MARGIN)] = key_grads(by_core(MARGIN + rows, 0), MARGIN).astype(BF16)
    back_inner.start()
    send_row(3, key_grads(MARGIN + own_rows[3], 1)[0])
    half = key_grads(MARGIN + near_half, MARGIN)
    back_inner.wait_recv()
    for i in range(MARGIN):
        send_row(1 + i, half[i] + rmar[i].astype(F32))
    last = key_grads(MARGIN + own_rows[4], 1)[0]
    for q in range(rows // 2):
        combine(q)
    relay_row(0)
    back_outer.wait_recv()
    send_row(4, last + rmar[MARGIN].astype(F32))
    for q in range(rows // 2, rows):
        combine(q)
    for k in (3, 1, 2):
        relay_row(k)

    def gap_is(other, side, distance):
        other = lax.rem(other + 2 * views, views)
        gap = other - partners[0, other] if side == 0 else partners[1, other] - other
        return jnp.where(lax.rem(gap + views, views) == distance, 1, 0)

    use = (
        gap_is(cam + step, 0, step),
        gap_is(cam - step, 1, step),
        gap_is(cam + 2 * step, 0, 2 * step),
        gap_is(cam - 2 * step, 1, 2 * step),
    )

    def arrived(k):
        for copy in relays(k):
            copy.wait_recv()
        summed = None
        for source in range(4):
            part = jnp.where(use[source] > 0, zin[source, k].astype(F32), 0.0)
            summed = part if summed is None else summed + part
        return summed

    xout[...] = arrived(0).astype(BF16)
    back_cross.start()
    relay_row(4)
    for k in (1, 2):
        both_out[1, own_rows[k]] = (own[own_rows[k]] + arrived(k)).astype(BF16)
    inside = own[own_rows[3]] + arrived(3)
    back_cross.wait_recv()
    both_out[1, own_rows[3]] = (inside + xin[...].astype(F32)).astype(BF16)
    both_out[1, own_rows[4]] = (own[own_rows[4]] + arrived(4)).astype(BF16)

    for copy in halo_outer:
        copy.wait_send()
    halo_inner.wait_send()
    sent = cand.at[:, pl.ds(0, n_inner + 2)]
    pltpu.make_async_copy(sent, sent, z_send).wait()
    for copy in (*margins, *crossing, back_inner, back_outer, back_cross):
        copy.wait_send()
    pltpu.make_async_copy(zin, zin, y_send).wait()


def local(
    views,
    slabs,
    features_in,
    conv_weight,
    q_weight,
    k_weight,
    v_weight,
    partners,
    band_widths,
    bands,
    grad_attended,
):
    _, rows, width, channels = features_in.shape
    block = (width, channels)
    chunks = rows + 1
    hbm = pl.BlockSpec(memory_space=pl.ANY)
    dma = pltpu.SemaphoreType.DMA
    out = jax.ShapeDtypeStruct((2, *features_in.shape[1:]), BF16)
    both = pl.pallas_call(
        functools.partial(kernel, views, slabs),
        out_shape=out,
        in_specs=[hbm] * 9,
        out_specs=pl.BlockSpec(memory_space=pltpu.VMEM),
        scratch_shapes=[
            pltpu.SMEM(partners.shape[::-1], jnp.int32),
            pltpu.SMEM(band_widths.shape[::-1], jnp.int32),
            pltpu.SMEM((1, *bands.shape[:0:-1]), jnp.int32),
            pltpu.VMEM((rows + 2 * MARGIN + 2, *block), BF16),
            pltpu.VMEM(conv_weight.shape, BF16),
            pltpu.VMEM(q_weight.shape, BF16),
            pltpu.VMEM(q_weight.shape, BF16),
            pltpu.VMEM(q_weight.shape, BF16),
            pltpu.VMEM((rows, *block), BF16),
            pltpu.VMEM((rows + 2 * MARGIN, *block), BF16),
            pltpu.VMEM((4, rows + 2 * MARGIN, *block), BF16),
            pltpu.VMEM((2, rows + 2 * MARGIN, *block), BF16),
            pltpu.VMEM((rows, 2 * width, channels), BF16),
            pltpu.VMEM((rows, 2 * BAND + 1, BLOCK, 2 * width), BF16),
            pltpu.VMEM((rows, *block), F32),
            pltpu.VMEM((MARGIN + 1, 2, *block), BF16),
            pltpu.VMEM((MARGIN + 1, 2, *block), BF16),
            pltpu.VMEM((2, chunks, *block), BF16),
            pltpu.VMEM((4, chunks, *block), BF16),
            pltpu.VMEM(block, BF16),
            pltpu.VMEM(block, BF16),
            dma((9,)),
            dma((3,)),
            dma((3,)),
            dma,
            dma((4, chunks)),
            dma((4,)),
            dma((4,)),
            dma((3,)),
            dma((3,)),
            dma,
            dma((4, chunks)),
        ],
        compiler_params=pltpu.CompilerParams(collective_id=0, has_side_effects=True, vmem_limit_bytes=32 << 20),
        name="views",
    )(
        *[
            pltpu.with_memory_space_constraint(array, pltpu.HBM)
            for array in (
                features_in,
                conv_weight,
                q_weight,
                k_weight,
                v_weight,
                partners.T,
                band_widths.T,
                bands.transpose(0, 3, 2, 1),
                grad_attended,
            )
        ]
    )
    return both[:1], both[1:]


def solution(mesh):
    placed = (
        P("cam", "row", None, None),
        P(),
        P(),
        P(),
        P(),
        P(),
        P(),
        P("cam", "row", None, None),
        P("cam", "row", None, None),
    )
    return jax.shard_map(
        functools.partial(local, mesh.shape["cam"], mesh.shape["row"]),
        mesh=mesh,
        in_specs=placed,
        out_specs=(P("cam", "row", None, None), P("cam", "row", None, None)),
        check_vma=False,
    )
```

```python
import functools

import jax
import jax.numpy as jnp
from jax import lax
from jax.experimental import pallas as pl
from jax.experimental.pallas import tpu as pltpu
from jax.sharding import PartitionSpec as P

MESH = pl.DeviceIdType.MESH
BLOCK = 128
MARGIN = 2
BAND = 3
F32 = jnp.float32
BF16 = jnp.bfloat16

NN = (((1,), (0,)), ((), ()))
NT = (((1,), (1,)), ((), ()))
TN = (((0,), (0,)), ((), ()))


def dot(a, b, dims=NN):
    return lax.dot_general(a, b, dims, preferred_element_type=F32)


def kernel(
    views,
    slabs,
    feat,
    conv_w,
    q_w,
    k_w,
    v_w,
    partners_in,
    widths_in,
    bands_in,
    grad_att,
    both_out,
    partners,
    widths,
    bands,
    fbuf,
    wconv,
    wq,
    wk,
    wv,
    dabuf,
    hwin,
    cand,
    wsel,
    qa,
    pd,
    own,
    gmar,
    rmar,
    ztot,
    zin,
    xout,
    xin,
    load_sem,
    o_send,
    halo_recv,
    z_send,
    z_recv,
    m_recv,
    b_recv,
    y_send,
    y_recv,
):
    step = views // min(16, views)
    rows = dabuf.shape[0]
    width, channels = dabuf.shape[1], dabuf.shape[2]
    reach = MARGIN + 1
    cam = lax.axis_index("cam")
    slab = lax.axis_index("row")
    cam_r, cam_l = lax.rem(cam + step, views), lax.rem(cam + views - step, views)
    odd = lax.rem(slab, 2)

    def by_core(even_value, odd_value):
        return even_value + (odd_value - even_value) * odd

    inner_slab = by_core(slab + 1, slab - 1)
    outer_slab = by_core(lax.rem(slab + slabs - 1, slabs), lax.rem(slab + 1, slabs))
    right, left = (cam_r, slab), (cam_l, slab)
    inner, outer = (cam, inner_slab), (cam, outer_slab)

    barrier = pltpu.get_barrier_semaphore()
    for peer in (outer, inner, right, left):
        pl.semaphore_signal(barrier, inc=1, device_id=peer, device_id_type=MESH)

    loads = [
        pltpu.make_async_copy(feat.at[0], fbuf.at[pl.ds(reach, rows)], load_sem.at[0]),
        pltpu.make_async_copy(conv_w, wconv, load_sem.at[1]),
        pltpu.make_async_copy(grad_att.at[0], dabuf, load_sem.at[2]),
        pltpu.make_async_copy(v_w, wv, load_sem.at[3]),
        pltpu.make_async_copy(q_w, wq, load_sem.at[4]),
        pltpu.make_async_copy(k_w, wk, load_sem.at[5]),
        pltpu.make_async_copy(partners_in, partners, load_sem.at[6]),
        pltpu.make_async_copy(widths_in, widths, load_sem.at[7]),
        pltpu.make_async_copy(bands_in, bands, load_sem.at[8]),
    ]
    for load in loads:
        load.start()

    def remote(src, dst, send, recv, peer):
        return pltpu.make_async_remote_copy(
            src_ref=src, dst_ref=dst, send_sem=send, recv_sem=recv, device_id=peer, device_id_type=MESH
        )

    halo_outer = [
        remote(
            feat.at[0, by_core(0, rows - 1)],
            fbuf.at[by_core(rows + reach, reach - 1)],
            o_send,
            halo_recv.at[0],
            outer,
        ),
        remote(
            feat.at[0, by_core(1, rows - MARGIN)],
            fbuf.at[by_core(rows + reach + 1, reach - MARGIN)],
            o_send,
            halo_recv.at[2],
            outer,
        ),
    ]
    halo_inner = remote(
        feat.at[0, by_core(rows - 1, 0)],
        fbuf.at[by_core(reach - 1, rows + reach)],
        o_send,
        halo_recv.at[1],
        inner,
    )
    edge_row = by_core(MARGIN + rows - 1, MARGIN)
    outer_row = by_core(MARGIN, MARGIN + rows - 1)
    margin_row = by_core(MARGIN - 1, MARGIN + rows)
    places = [by_core(MARGIN + 1, MARGIN + 2), by_core(MARGIN + 2, MARGIN + 1), edge_row, outer_row, margin_row]
    n_inner = rows - 1

    def near(k):
        r = places[k]
        return (
            remote(hwin.at[r], cand.at[0, r], z_send, z_recv.at[0, k], right),
            remote(hwin.at[r], cand.at[2, r], z_send, z_recv.at[2, k], left),
        )

    def far(k):
        r = places[k]
        return (
            remote(cand.at[0, r], cand.at[1, r], z_send, z_recv.at[1, k], right),
            remote(cand.at[2, r], cand.at[3, r], z_send, z_recv.at[3, k], left),
        )

    def conv(start, count):
        total = None
        for dy in range(3):
            weight = jnp.concatenate([wconv[dy, 0], wconv[dy, 1], wconv[dy, 2]], axis=1)
            tap = fbuf[pl.ds(start + dy, count)].reshape(count * width, channels)
            part = dot(tap, weight)
            total = part if total is None else total + part
        size = count * width
        pixel = lax.rem(lax.broadcasted_iota(jnp.int32, (size, channels), 0), width)
        before = pltpu.roll(total[:, :channels], 1, 0)
        after = pltpu.roll(total[:, 2 * channels :], size - 1, 0)
        out = total[:, channels : 2 * channels]
        out = out + jnp.where(pixel == 0, 0.0, before) + jnp.where(pixel == width - 1, 0.0, after)
        hwin[pl.ds(start, count)] = out.astype(BF16).reshape(count, width, channels)

    def relay(ks):
        for k in ks:
            for near_copy, far_copy in zip(near(k), far(k)):
                near_copy.wait_recv()
                far_copy.start()

    def launch(ks):
        for k in ks:
            for copy in near(k):
                copy.start()

    loads[0].wait()
    loads[1].wait()
    conv(MARGIN + 1, rows - 2)
    pl.semaphore_wait(barrier, 4)
    halo_outer[0].start()
    halo_inner.start()
    halo_outer[1].start()
    launch(range(rows - 2))

    loads[2].wait()
    loads[3].wait()
    loads[4].wait()
    loads[5].wait()
    grad_v = dot(dabuf[...].reshape(rows * width, channels), wv[...], NT).astype(BF16)
    qa[:, pl.ds(width, width), :] = grad_v.reshape(rows, width, channels)
    pd[:, 2 * BAND] = jnp.zeros((rows, BLOCK, 2 * width), BF16)

    halo_inner.wait_recv()
    conv(edge_row, 1)
    launch([rows - 2])
    relay([0])
    halo_outer[0].wait_recv()

    @pl.when(jnp.logical_or(slab == 0, slab == slabs - 1))
    def _():
        fbuf[by_core(reach - 1, rows + reach)] = jnp.zeros((width, channels), BF16)

    conv(outer_row, 1)
    launch([n_inner])
    halo_outer[1].wait_recv()
    conv(margin_row, 1)
    launch([n_inner + 1])
    relay(range(1, n_inner))

    scale = channels**-0.5
    queries = dot(hwin[pl.ds(MARGIN, rows)].reshape(rows * width, channels), wq[...]).astype(BF16)
    queries = (dot(queries, wk[...], NT) * scale).astype(BF16)
    qa[:, pl.ds(0, width), :] = queries.reshape(rows, width, channels)

    for load in loads[6:]:
        load.wait()
    gap0 = lax.rem(cam - partners[0, cam] + views, views)
    gap1 = lax.rem(partners[1, cam] - cam + views, views)

    def select(ks):
        for k in ks:
            r = places[k]
            for copy in far(k):
                copy.wait_recv()
            wsel[0, r] = jnp.where(gap0 == step, cand[0, r], cand[1, r])
            wsel[1, r] = jnp.where(gap1 == step, cand[2, r], cand[3, r])

    select([0])
    crossing = [
        remote(
            wsel.at[side, places[0]],
            wsel.at[side, by_core(2 * MARGIN + rows - 1, 0)],
            o_send,
            m_recv.at[2 + side],
            outer,
        )
        for side in range(2)
    ]
    for copy in crossing:
        copy.start()
    relay(range(n_inner, n_inner + 2))
    select(range(1, n_inner))
    mine = pl.ds(by_core(rows, MARGIN), MARGIN)
    theirs = pl.ds(by_core(0, MARGIN + rows), MARGIN)
    margins = [
        remote(wsel.at[side, mine], wsel.at[side, theirs], o_send, m_recv.at[side], inner)
        for side in range(2)
    ]
    for copy in margins:
        copy.start()
    select(range(n_inner, n_inner + 2))
    for copy in (*margins, *crossing):
        copy.wait_recv()

    base = slab * rows - MARGIN

    def key_block(q, side, slot):
        return wsel[side, jnp.clip(bands[0, slot, side, q] - base, 0, rows + 2 * MARGIN - 1)]

    lists = [(side, slot) for side in range(2) for slot in range(BAND)]

    def attend(q):
        qa_here = qa[q]
        exps, grads = [], []
        total, weighted = None, None
        for side, slot in lists:
            both = dot(key_block(q, side, slot), qa_here, NT)
            expo = jnp.where(slot < widths[side, cam], jnp.exp(both[:, :width]), 0.0)
            grad = both[:, width:]
            exps.append(expo)
            grads.append(grad)
            here = jnp.sum(expo, axis=0, keepdims=True)
            here_w = jnp.sum(expo * grad, axis=0, keepdims=True)
            total = here if total is None else total + here
            weighted = here_w if weighted is None else weighted + here_w
        inverse = 1.0 / total
        delta = weighted * inverse
        for place in range(2 * BAND):
            prob = exps[place] * inverse
            score = prob * (grads[place] - delta)
            pd[q, place] = jnp.concatenate([score.astype(BF16), prob.astype(BF16)], axis=1)

    def combine(q):
        keys = jnp.concatenate([key_block(q, side, slot) for side, slot in lists], axis=0)
        pairs = pd[q, pl.ds(0, 2 * BAND)].reshape(2 * BAND * BLOCK, 2 * width)
        mixed = dot(keys, pairs, TN).astype(BF16)
        both_out[0, q] = dot(mixed[:, width:], wv[...], TN).astype(BF16)
        grad_q = (dot(mixed[:, :width], wk[...], TN) * scale).astype(BF16)
        own[q] = dot(grad_q, wq[...], NT)

    for q in range(rows):
        attend(q)

    def place_of(q, side, row):
        place = jnp.int32(2 * BAND)
        for slot in range(BAND):
            place = jnp.where(bands[0, slot, side, q] - base == row, side * BAND + slot, place)
        return place

    def key_grads(first, count):
        summed = None
        for q in range(rows):
            lhs = jnp.concatenate(
                [pd[q, place_of(q, side, first + i)] for i in range(count) for side in range(2)], axis=0
            )
            part = dot(lhs, qa[q])
            summed = part if summed is None else summed + part
        return summed.reshape(count, 2, BLOCK, channels)

    near_half = by_core(MARGIN, 0)
    own_rows = [None, near_half, near_half + 1, by_core(1, rows - MARGIN), by_core(0, rows - 1)]
    back_inner = remote(gmar.at[pl.ds(0, MARGIN)], rmar.at[pl.ds(0, MARGIN)], o_send, b_recv.at[0], inner)
    back_outer = remote(gmar.at[MARGIN], rmar.at[MARGIN], o_send, b_recv.at[1], outer)
    back_cross = remote(xout, xin, o_send, b_recv.at[2], outer)

    def totals(k):
        return (
            remote(ztot.at[0, k], zin.at[0, k], y_send, y_recv.at[0, k], left),
            remote(ztot.at[1, k], zin.at[1, k], y_send, y_recv.at[1, k], right),
        )

    def relays(k):
        return (
            remote(zin.at[0, k], zin.at[2, k], y_send, y_recv.at[2, k], left),
            remote(zin.at[1, k], zin.at[3, k], y_send, y_recv.at[3, k], right),
        )

    def send_row(k, summed):
        ztot[:, k] = summed.astype(BF16)
        for copy in totals(k):
            copy.start()

    def relay_row(k):
        for copy, onward in zip(totals(k), relays(k)):
            copy.wait_recv()
            onward.start()

    gmar[MARGIN] = key_grads(by_core(MARGIN - 1, MARGIN + rows), 1)[0].astype(BF16)
    back_outer.start()
    send_row(0, key_grads(by_core(0, 2 * MARGIN + rows - 1), 1)[0])
    gmar[pl.ds(0, MARGIN)] = key_grads(by_core(MARGIN + rows, 0), MARGIN).astype(BF16)
    back_inner.start()
    send_row(3, key_grads(MARGIN + own_rows[3], 1)[0])
    half = key_grads(MARGIN + near_half, MARGIN)
    back_inner.wait_recv()
    for i in range(MARGIN):
        send_row(1 + i, half[i] + rmar[i].astype(F32))
    last = key_grads(MARGIN + own_rows[4], 1)[0]
    for q in range(rows // 2):
        combine(q)
    relay_row(0)
    back_outer.wait_recv()
    send_row(4, last + rmar[MARGIN].astype(F32))
    for q in range(rows // 2, rows):
        combine(q)
    for k in (3, 1, 2):
        relay_row(k)

    def gap_is(other, side, distance):
        other = lax.rem(other + 2 * views, views)
        gap = other - partners[0, other] if side == 0 else partners[1, other] - other
        return jnp.where(lax.rem(gap + views, views) == distance, 1, 0)

    use = (
        gap_is(cam + step, 0, step),
        gap_is(cam - step, 1, step),
        gap_is(cam + 2 * step, 0, 2 * step),
        gap_is(cam - 2 * step, 1, 2 * step),
    )

    def arrived(k):
        for copy in relays(k):
            copy.wait_recv()
        summed = None
        for source in range(4):
            part = jnp.where(use[source] > 0, zin[source, k].astype(F32), 0.0)
            summed = part if summed is None else summed + part
        return summed

    xout[...] = arrived(0).astype(BF16)
    back_cross.start()
    relay_row(4)
    for k in (1, 2):
        both_out[1, own_rows[k]] = (own[own_rows[k]] + arrived(k)).astype(BF16)
    inside = own[own_rows[3]] + arrived(3)
    back_cross.wait_recv()
    both_out[1, own_rows[3]] = (inside + xin[...].astype(F32)).astype(BF16)
    both_out[1, own_rows[4]] = (own[own_rows[4]] + arrived(4)).astype(BF16)

    others = cand.at[:, pl.ds(0, rows)]
    pltpu.make_async_copy(others, others, o_send).wait()
    sent = cand.at[:, pl.ds(0, n_inner + 2)]
    pltpu.make_async_copy(sent, sent, z_send).wait()
    pltpu.make_async_copy(zin, zin, y_send).wait()


def local(
    views,
    slabs,
    features_in,
    conv_weight,
    q_weight,
    k_weight,
    v_weight,
    partners,
    band_widths,
    bands,
    grad_attended,
):
    _, rows, width, channels = features_in.shape
    block = (width, channels)
    chunks = rows + 1
    hbm = pl.BlockSpec(memory_space=pl.ANY)
    dma = pltpu.SemaphoreType.DMA
    out = jax.ShapeDtypeStruct((2, *features_in.shape[1:]), BF16)
    both = pl.pallas_call(
        functools.partial(kernel, views, slabs),
        out_shape=out,
        in_specs=[hbm] * 9,
        out_specs=pl.BlockSpec(memory_space=pltpu.VMEM),
        scratch_shapes=[
            pltpu.SMEM(partners.shape[::-1], jnp.int32),
            pltpu.SMEM(band_widths.shape[::-1], jnp.int32),
            pltpu.SMEM((1, *bands.shape[:0:-1]), jnp.int32),
            pltpu.VMEM((rows + 2 * MARGIN + 2, *block), BF16),
            pltpu.VMEM(conv_weight.shape, BF16),
            pltpu.VMEM(q_weight.shape, BF16),
            pltpu.VMEM(q_weight.shape, BF16),
            pltpu.VMEM(q_weight.shape, BF16),
            pltpu.VMEM((rows, *block), BF16),
            pltpu.VMEM((rows + 2 * MARGIN, *block), BF16),
            pltpu.VMEM((4, rows + 2 * MARGIN, *block), BF16),
            pltpu.VMEM((2, rows + 2 * MARGIN, *block), BF16),
            pltpu.VMEM((rows, 2 * width, channels), BF16),
            pltpu.VMEM((rows, 2 * BAND + 1, BLOCK, 2 * width), BF16),
            pltpu.VMEM((rows, *block), F32),
            pltpu.VMEM((MARGIN + 1, 2, *block), BF16),
            pltpu.VMEM((MARGIN + 1, 2, *block), BF16),
            pltpu.VMEM((2, chunks, *block), BF16),
            pltpu.VMEM((4, chunks, *block), BF16),
            pltpu.VMEM(block, BF16),
            pltpu.VMEM(block, BF16),
            dma((9,)),
            dma,
            dma((3,)),
            dma,
            dma((4, chunks)),
            dma((4,)),
            dma((3,)),
            dma,
            dma((4, chunks)),
        ],
        compiler_params=pltpu.CompilerParams(collective_id=0, has_side_effects=True, vmem_limit_bytes=32 << 20),
        name="views",
    )(
        *[
            pltpu.with_memory_space_constraint(array, pltpu.HBM)
            for array in (
                features_in,
                conv_weight,
                q_weight,
                k_weight,
                v_weight,
                partners.T,
                band_widths.T,
                bands.transpose(0, 3, 2, 1),
                grad_attended,
            )
        ]
    )
    return both[:1], both[1:]


def solution(mesh):
    placed = (
        P("cam", "row", None, None),
        P(),
        P(),
        P(),
        P(),
        P(),
        P(),
        P("cam", "row", None, None),
        P("cam", "row", None, None),
    )
    return jax.shard_map(
        functools.partial(local, mesh.shape["cam"], mesh.shape["row"]),
        mesh=mesh,
        in_specs=placed,
        out_specs=(P("cam", "row", None, None), P("cam", "row", None, None)),
        check_vma=False,
    )
```

```python
import functools

import jax
import jax.numpy as jnp
from jax import lax
from jax.experimental import pallas as pl
from jax.experimental.pallas import tpu as pltpu
from jax.sharding import PartitionSpec as P

MESH = pl.DeviceIdType.MESH
BLOCK = 128
MARGIN = 2
BAND = 3
F32 = jnp.float32
BF16 = jnp.bfloat16

NN = (((1,), (0,)), ((), ()))
NT = (((1,), (1,)), ((), ()))
TN = (((0,), (0,)), ((), ()))


def dot(a, b, dims=NN):
    return lax.dot_general(a, b, dims, preferred_element_type=F32)


def kernel(
    views,
    slabs,
    feat,
    conv_w,
    q_w,
    k_w,
    v_w,
    partners_in,
    widths_in,
    bands_in,
    grad_att,
    both_out,
    partners,
    widths,
    bands,
    fbuf,
    wconv,
    wq,
    wk,
    wv,
    dabuf,
    hwin,
    cand,
    wsel,
    qa,
    pd,
    own,
    gmar,
    rmar,
    ztot,
    zin,
    xout,
    xin,
    load_sem,
    o_send,
    halo_recv,
    z_send,
    z_recv,
    m_recv,
    b_recv,
    y_send,
    y_recv,
):
    step = views // min(16, views)
    rows = dabuf.shape[0]
    width, channels = dabuf.shape[1], dabuf.shape[2]
    reach = MARGIN + 1
    cam = lax.axis_index("cam")
    slab = lax.axis_index("row")
    cam_r, cam_l = lax.rem(cam + step, views), lax.rem(cam + views - step, views)
    odd = lax.rem(slab, 2)

    def by_core(even_value, odd_value):
        return even_value + (odd_value - even_value) * odd

    inner_slab = by_core(slab + 1, slab - 1)
    outer_slab = by_core(lax.rem(slab + slabs - 1, slabs), lax.rem(slab + 1, slabs))
    right, left = (cam_r, slab), (cam_l, slab)
    inner, outer = (cam, inner_slab), (cam, outer_slab)

    barrier = pltpu.get_barrier_semaphore()
    for peer in (outer, inner, right, left):
        pl.semaphore_signal(barrier, inc=1, device_id=peer, device_id_type=MESH)

    loads = [
        pltpu.make_async_copy(feat.at[0], fbuf.at[pl.ds(reach, rows)], load_sem.at[0]),
        pltpu.make_async_copy(conv_w, wconv, load_sem.at[1]),
        pltpu.make_async_copy(grad_att.at[0], dabuf, load_sem.at[2]),
        pltpu.make_async_copy(v_w, wv, load_sem.at[3]),
        pltpu.make_async_copy(q_w, wq, load_sem.at[4]),
        pltpu.make_async_copy(k_w, wk, load_sem.at[5]),
        pltpu.make_async_copy(partners_in, partners, load_sem.at[6]),
        pltpu.make_async_copy(widths_in, widths, load_sem.at[7]),
        pltpu.make_async_copy(bands_in, bands, load_sem.at[8]),
    ]
    for load in loads:
        load.start()

    def remote(src, dst, send, recv, peer):
        return pltpu.make_async_remote_copy(
            src_ref=src, dst_ref=dst, send_sem=send, recv_sem=recv, device_id=peer, device_id_type=MESH
        )

    halo_outer = [
        remote(
            feat.at[0, by_core(0, rows - 1)],
            fbuf.at[by_core(rows + reach, reach - 1)],
            o_send,
            halo_recv.at[0],
            outer,
        ),
        remote(
            feat.at[0, by_core(1, rows - MARGIN)],
            fbuf.at[by_core(rows + reach + 1, reach - MARGIN)],
            o_send,
            halo_recv.at[2],
            outer,
        ),
    ]
    halo_inner = remote(
        feat.at[0, by_core(rows - 1, 0)],
        fbuf.at[by_core(reach - 1, rows + reach)],
        o_send,
        halo_recv.at[1],
        inner,
    )
    edge_row = by_core(MARGIN + rows - 1, MARGIN)
    outer_row = by_core(MARGIN, MARGIN + rows - 1)
    margin_row = by_core(MARGIN - 1, MARGIN + rows)
    places = [by_core(MARGIN + 1, MARGIN + 2), by_core(MARGIN + 2, MARGIN + 1), edge_row, outer_row, margin_row]
    n_inner = rows - 1

    def near(k):
        r = places[k]
        return (
            remote(hwin.at[r], cand.at[0, r], z_send, z_recv.at[0, k], right),
            remote(hwin.at[r], cand.at[2, r], z_send, z_recv.at[2, k], left),
        )

    def far(k):
        r = places[k]
        return (
            remote(cand.at[0, r], cand.at[1, r], z_send, z_recv.at[1, k], right),
            remote(cand.at[2, r], cand.at[3, r], z_send, z_recv.at[3, k], left),
        )

    def conv(start, count):
        total = None
        for dy in range(3):
            weight = jnp.concatenate([wconv[dy, 0], wconv[dy, 1], wconv[dy, 2]], axis=1)
            tap = fbuf[pl.ds(start + dy, count)].reshape(count * width, channels)
            part = dot(tap, weight)
            total = part if total is None else total + part
        size = count * width
        pixel = lax.rem(lax.broadcasted_iota(jnp.int32, (size, channels), 0), width)
        before = pltpu.roll(total[:, :channels], 1, 0)
        after = pltpu.roll(total[:, 2 * channels :], size - 1, 0)
        out = total[:, channels : 2 * channels]
        out = out + jnp.where(pixel == 0, 0.0, before) + jnp.where(pixel == width - 1, 0.0, after)
        hwin[pl.ds(start, count)] = out.astype(BF16).reshape(count, width, channels)

    def relay(ks):
        for k in ks:
            for near_copy, far_copy in zip(near(k), far(k)):
                near_copy.wait_recv()
                far_copy.start()

    def launch(ks):
        for k in ks:
            for copy in near(k):
                copy.start()

    loads[0].wait()
    loads[1].wait()
    conv(MARGIN + 1, rows - 2)
    pl.semaphore_wait(barrier, 4)
    halo_outer[0].start()
    halo_inner.start()
    halo_outer[1].start()
    launch(range(rows - 2))

    loads[2].wait()
    loads[3].wait()
    loads[4].wait()
    loads[5].wait()
    grad_v = dot(dabuf[...].reshape(rows * width, channels), wv[...], NT).astype(BF16)
    qa[:, pl.ds(width, width), :] = grad_v.reshape(rows, width, channels)
    pd[:, 2 * BAND] = jnp.zeros((rows, BLOCK, 2 * width), BF16)

    halo_inner.wait_recv()
    conv(edge_row, 1)
    launch([rows - 2])
    relay([0])
    halo_outer[0].wait_recv()

    @pl.when(jnp.logical_or(slab == 0, slab == slabs - 1))
    def _():
        fbuf[by_core(reach - 1, rows + reach)] = jnp.zeros((width, channels), BF16)

    conv(outer_row, 1)
    launch([n_inner])
    halo_outer[1].wait_recv()
    conv(margin_row, 1)
    launch([n_inner + 1])
    relay(range(1, n_inner))

    scale = channels**-0.5
    queries = dot(hwin[pl.ds(MARGIN, rows)].reshape(rows * width, channels), wq[...]).astype(BF16)
    queries = (dot(queries, wk[...], NT) * scale).astype(BF16)
    qa[:, pl.ds(0, width), :] = queries.reshape(rows, width, channels)

    for load in loads[6:]:
        load.wait()
    gap0 = lax.rem(cam - partners[0, cam] + views, views)
    gap1 = lax.rem(partners[1, cam] - cam + views, views)

    def select(ks):
        for k in ks:
            r = places[k]
            for copy in far(k):
                copy.wait_recv()
            wsel[0, r] = jnp.where(gap0 == step, cand[0, r], cand[1, r])
            wsel[1, r] = jnp.where(gap1 == step, cand[2, r], cand[3, r])

    select([0])
    crossing = [
        remote(
            wsel.at[side, places[0]],
            wsel.at[side, by_core(2 * MARGIN + rows - 1, 0)],
            o_send,
            m_recv.at[2 + side],
            outer,
        )
        for side in range(2)
    ]
    for copy in crossing:
        copy.start()
    relay(range(n_inner, n_inner + 2))
    select(range(1, n_inner))
    mine = pl.ds(by_core(rows, MARGIN), MARGIN)
    theirs = pl.ds(by_core(0, MARGIN + rows), MARGIN)
    margins = [
        remote(wsel.at[side, mine], wsel.at[side, theirs], o_send, m_recv.at[side], inner)
        for side in range(2)
    ]
    for copy in margins:
        copy.start()
    select(range(n_inner, n_inner + 2))
    for copy in (*margins, *crossing):
        copy.wait_recv()

    base = slab * rows - MARGIN

    def key_block(q, side, slot):
        return wsel[side, jnp.clip(bands[0, slot, side, q] - base, 0, rows + 2 * MARGIN - 1)]

    lists = [(side, slot) for side in range(2) for slot in range(BAND)]

    def attend(q):
        qa_here = qa[q]
        exps, grads = [], []
        total, weighted = None, None
        for side, slot in lists:
            both = dot(key_block(q, side, slot), qa_here, NT)
            expo = jnp.where(slot < widths[side, cam], jnp.exp(both[:, :width]), 0.0)
            grad = both[:, width:]
            exps.append(expo)
            grads.append(grad)
            here = jnp.sum(expo, axis=0, keepdims=True)
            here_w = jnp.sum(expo * grad, axis=0, keepdims=True)
            total = here if total is None else total + here
            weighted = here_w if weighted is None else weighted + here_w
        inverse = 1.0 / total
        delta = weighted * inverse
        for place in range(2 * BAND):
            prob = exps[place] * inverse
            score = prob * (grads[place] - delta)
            pd[q, place] = jnp.concatenate([score.astype(BF16), prob.astype(BF16)], axis=1)

    def combine(q):
        keys = jnp.concatenate([key_block(q, side, slot) for side, slot in lists], axis=0)
        pairs = pd[q, pl.ds(0, 2 * BAND)].reshape(2 * BAND * BLOCK, 2 * width)
        mixed = dot(keys, pairs, TN).astype(BF16)
        both_out[0, q] = dot(mixed[:, width:], wv[...], TN).astype(BF16)
        grad_q = (dot(mixed[:, :width], wk[...], TN) * scale).astype(BF16)
        own[q] = dot(grad_q, wq[...], NT)

    for q in range(rows):
        attend(q)

    def place_of(q, side, row):
        place = jnp.int32(2 * BAND)
        for slot in range(BAND):
            place = jnp.where(bands[0, slot, side, q] - base == row, side * BAND + slot, place)
        return place

    def key_grads(first, count):
        summed = None
        for q in range(rows):
            lhs = jnp.concatenate(
                [pd[q, place_of(q, side, first + i)] for i in range(count) for side in range(2)], axis=0
            )
            part = dot(lhs, qa[q])
            summed = part if summed is None else summed + part
        return summed.reshape(count, 2, BLOCK, channels)

    near_half = by_core(MARGIN, 0)
    own_rows = [None, near_half, near_half + 1, by_core(1, rows - MARGIN), by_core(0, rows - 1)]
    back_inner = remote(gmar.at[pl.ds(0, MARGIN)], rmar.at[pl.ds(0, MARGIN)], o_send, b_recv.at[0], inner)
    back_outer = remote(gmar.at[MARGIN], rmar.at[MARGIN], o_send, b_recv.at[1], outer)
    back_cross = remote(xout, xin, o_send, b_recv.at[2], outer)

    def totals(k):
        return (
            remote(ztot.at[0, k], zin.at[0, k], y_send, y_recv.at[0, k], left),
            remote(ztot.at[1, k], zin.at[1, k], y_send, y_recv.at[1, k], right),
        )

    def relays(k):
        return (
            remote(zin.at[0, k], zin.at[2, k], y_send, y_recv.at[2, k], left),
            remote(zin.at[1, k], zin.at[3, k], y_send, y_recv.at[3, k], right),
        )

    def send_row(k, summed):
        ztot[:, k] = summed.astype(BF16)
        for copy in totals(k):
            copy.start()

    def relay_row(k):
        for copy, onward in zip(totals(k), relays(k)):
            copy.wait_recv()
            onward.start()

    send_row(0, key_grads(by_core(0, 2 * MARGIN + rows - 1), 1)[0])
    gmar[MARGIN] = key_grads(by_core(MARGIN - 1, MARGIN + rows), 1)[0].astype(BF16)
    back_outer.start()
    gmar[pl.ds(0, MARGIN)] = key_grads(by_core(MARGIN + rows, 0), MARGIN).astype(BF16)
    back_inner.start()
    send_row(3, key_grads(MARGIN + own_rows[3], 1)[0])
    half = key_grads(MARGIN + near_half, MARGIN)
    back_inner.wait_recv()
    for i in range(MARGIN):
        send_row(1 + i, half[i] + rmar[i].astype(F32))
    last = key_grads(MARGIN + own_rows[4], 1)[0]
    for q in range(rows // 2):
        combine(q)
    relay_row(0)
    back_outer.wait_recv()
    send_row(4, last + rmar[MARGIN].astype(F32))
    for q in range(rows // 2, rows):
        combine(q)
    for k in (3, 1, 2):
        relay_row(k)

    def gap_is(other, side, distance):
        other = lax.rem(other + 2 * views, views)
        gap = other - partners[0, other] if side == 0 else partners[1, other] - other
        return jnp.where(lax.rem(gap + views, views) == distance, 1, 0)

    use = (
        gap_is(cam + step, 0, step),
        gap_is(cam - step, 1, step),
        gap_is(cam + 2 * step, 0, 2 * step),
        gap_is(cam - 2 * step, 1, 2 * step),
    )

    def arrived(k):
        for copy in relays(k):
            copy.wait_recv()
        summed = None
        for source in range(4):
            part = jnp.where(use[source] > 0, zin[source, k].astype(F32), 0.0)
            summed = part if summed is None else summed + part
        return summed

    xout[...] = arrived(0).astype(BF16)
    back_cross.start()
    relay_row(4)
    for k in (1, 2):
        both_out[1, own_rows[k]] = (own[own_rows[k]] + arrived(k)).astype(BF16)
    inside = own[own_rows[3]] + arrived(3)
    back_cross.wait_recv()
    both_out[1, own_rows[3]] = (inside + xin[...].astype(F32)).astype(BF16)
    both_out[1, own_rows[4]] = (own[own_rows[4]] + arrived(4)).astype(BF16)

    others = cand.at[:, pl.ds(0, rows)]
    pltpu.make_async_copy(others, others, o_send).wait()
    sent = cand.at[:, pl.ds(0, n_inner + 2)]
    pltpu.make_async_copy(sent, sent, z_send).wait()
    pltpu.make_async_copy(zin, zin, y_send).wait()


def local(
    views,
    slabs,
    features_in,
    conv_weight,
    q_weight,
    k_weight,
    v_weight,
    partners,
    band_widths,
    bands,
    grad_attended,
):
    _, rows, width, channels = features_in.shape
    block = (width, channels)
    chunks = rows + 1
    hbm = pl.BlockSpec(memory_space=pl.ANY)
    dma = pltpu.SemaphoreType.DMA
    out = jax.ShapeDtypeStruct((2, *features_in.shape[1:]), BF16)
    both = pl.pallas_call(
        functools.partial(kernel, views, slabs),
        out_shape=out,
        in_specs=[hbm] * 9,
        out_specs=pl.BlockSpec(memory_space=pltpu.VMEM),
        scratch_shapes=[
            pltpu.SMEM(partners.shape[::-1], jnp.int32),
            pltpu.SMEM(band_widths.shape[::-1], jnp.int32),
            pltpu.SMEM((1, *bands.shape[:0:-1]), jnp.int32),
            pltpu.VMEM((rows + 2 * MARGIN + 2, *block), BF16),
            pltpu.VMEM(conv_weight.shape, BF16),
            pltpu.VMEM(q_weight.shape, BF16),
            pltpu.VMEM(q_weight.shape, BF16),
            pltpu.VMEM(q_weight.shape, BF16),
            pltpu.VMEM((rows, *block), BF16),
            pltpu.VMEM((rows + 2 * MARGIN, *block), BF16),
            pltpu.VMEM((4, rows + 2 * MARGIN, *block), BF16),
            pltpu.VMEM((2, rows + 2 * MARGIN, *block), BF16),
            pltpu.VMEM((rows, 2 * width, channels), BF16),
            pltpu.VMEM((rows, 2 * BAND + 1, BLOCK, 2 * width), BF16),
            pltpu.VMEM((rows, *block), F32),
            pltpu.VMEM((MARGIN + 1, 2, *block), BF16),
            pltpu.VMEM((MARGIN + 1, 2, *block), BF16),
            pltpu.VMEM((2, chunks, *block), BF16),
            pltpu.VMEM((4, chunks, *block), BF16),
            pltpu.VMEM(block, BF16),
            pltpu.VMEM(block, BF16),
            dma((9,)),
            dma,
            dma((3,)),
            dma,
            dma((4, chunks)),
            dma((4,)),
            dma((3,)),
            dma,
            dma((4, chunks)),
        ],
        compiler_params=pltpu.CompilerParams(collective_id=0, has_side_effects=True, vmem_limit_bytes=32 << 20),
        name="views",
    )(
        *[
            pltpu.with_memory_space_constraint(array, pltpu.HBM)
            for array in (
                features_in,
                conv_weight,
                q_weight,
                k_weight,
                v_weight,
                partners.T,
                band_widths.T,
                bands.transpose(0, 3, 2, 1),
                grad_attended,
            )
        ]
    )
    return both[:1], both[1:]


def solution(mesh):
    placed = (
        P("cam", "row", None, None),
        P(),
        P(),
        P(),
        P(),
        P(),
        P(),
        P("cam", "row", None, None),
        P("cam", "row", None, None),
    )
    return jax.shard_map(
        functools.partial(local, mesh.shape["cam"], mesh.shape["row"]),
        mesh=mesh,
        in_specs=placed,
        out_specs=(P("cam", "row", None, None), P("cam", "row", None, None)),
        check_vma=False,
    )
```
